32 devices in a mesh: row: 4 (over y, core), col: 8 (over z, x).
Axes of the slice: x: 2, y: 2, z: 4, core: 2. Of those that a mesh axis runs over, the one named last changes fastest.
Arguments:
- inverse: float32 [16384, 16384], P('row', 'col'), may hold values from -6 to 6
- front_blocks: int32 [2, 16], replicated, may hold values from 0 to 63, as said below
- panels: float32 [2, 4096, 256], P(None, 'row'), may hold values from -0.09375 to 0.09375
- diag_terms: float32 [2, 256, 256], replicated, may hold values from -6 to 6
- bounds: int32 [2, 4], replicated, may hold values from 1 to 128, 256 in all within a row
Outputs:
- border: float32 [2, 4096, 256], P(None, ('row', 'col'))
- diag_block: float32 [2, 256, 256], replicated
The draws below stay inside these ranges and needn't reach their ends.
Inputs may be any that keep to these rules, and one draw needn't show every extreme that they name: `front_blocks`: each row names 16 distinct blocks. Positions 4 r to 4 r + 3 name blocks of four different groups of 16 consecutive blocks, and every such group is named at exactly four positions, of four different r. Positions 2 o and 2 o + 1 name blocks of two different groups of 8 consecutive blocks, and every such group is named at exactly two positions, of two different o.
All inputs are finite; a program needn't handle non-finite values.
Results may differ from the reference program's by a relative error of at most 0.0001.
Values sent between devices are 32-bit elements; how exact they have to be, the bound alone decides.
A program may use at most 128 MiB of HBM per device.

```python
import math
import jax
import jax.numpy as jnp
import numpy as np
from jax import lax

ORDER = 16384
BS = 256
PC = 256
NSUP = 4
FRONTS = 2
KB = 16
MF = 4096
N_ROW = 4
N_COL = 8


def draw_front_blocks(key, part):
    block_count = ORDER // BS
    group_size = block_count // N_COL
    chosen_rows = []
    for front_index in range(2):
        front_key = jax.random.fold_in(key, 101 + front_index)
        subkeys = jax.random.split(front_key, 4)
        order_rows = jax.random.permutation(subkeys[0], N_ROW)
        offset = jax.random.randint(subkeys[1], (), 0, N_ROW)
        flip_bits = jax.random.randint(subkeys[2], (N_ROW,), 0, 2)
        within = jax.vmap(lambda subkey: jax.random.permutation(subkey, group_size))(jax.random.split(subkeys[3], N_COL))
        position = jnp.arange(KB)
        holder = position // 2
        second = position % 2
        row_holder = holder // 2
        shift_step = 2 * (holder % 2) + second
        region = order_rows[(row_holder + offset + shift_step) % N_ROW]
        column_group = 2 * region + (second + flip_bits[region]) % 2
        chosen = column_group * group_size + within[column_group, holder % 2]
        chosen_rows.append(chosen)
    return jnp.stack(chosen_rows).astype(jnp.int32)


def steps_of(key, shape, cuts, low, largest):
    def one(axis_at, blocks):
        heights = jax.random.uniform(jax.random.fold_in(jax.random.fold_in(key, 6), axis_at), (blocks,), jnp.float32, low / len(cuts), largest / len(cuts))
        return jnp.repeat(jnp.exp(heights), shape[axis_at] // blocks).reshape((-1,) + (1,) * (len(shape) - axis_at - 1))

    gain = one(*cuts[0])
    for cut in cuts[1:]:
        gain = gain * one(*cut)
    return gain


def profile(count, total, reach, slope):
    loads = [(1 << 20) // math.isqrt(standing ** slope) + 1 for standing in range(2, count + 1)]
    spare, holding = total - reach - (count - 1), [1] * (count - 1)
    while spare > 0:
        movable = [i for i in range(count - 1) if holding[i] < reach]
        mass, left = sum([loads[i] for i in movable]), spare
        for i in movable:
            extra = min(reach - holding[i], max(1, left * loads[i] // mass), spare)
            holding[i] = holding[i] + extra
            spare = spare - extra
    return np.array([reach] + holding)


def uneven(key, amount, total, most, skew):
    if amount == 2:
        one = jax.random.randint(key, (), max(1, total - most), min(most, total - 1) + 1)
        return jnp.stack([one, total - one])
    sizes = jnp.asarray(profile(amount, total, most, skew), jnp.int32)
    twos = (amount - 1) // 2
    donor, taker = sizes[1:1 + 2 * twos:2], sizes[2:2 + 2 * twos:2]
    margin = jnp.minimum(donor - 1, most - taker)
    passed = jax.random.randint(jax.random.fold_in(key, 1), (twos,), 0, 1 << 20) % (margin + 1)
    sizes = sizes.at[1:1 + 2 * twos:2].set(donor - passed).at[2:2 + 2 * twos:2].set(taker + passed)
    return sizes[jax.random.permutation(jax.random.fold_in(key, 2), amount)]


def centred(rng, extent, spread, bound, shards=(), held_as=jnp.bfloat16):
    values = jax.random.normal(rng, extent, jnp.float32) * spread
    if len(shards) > 0:
        values = steps_of(rng, extent, shards, -0.22, 0.18) * values
    return jnp.clip(values, min=-bound, max=bound).astype(held_as)


def setup_inputs(seed: int = 0) -> dict:
    key_of = jax.random.split(jax.random.key(seed), 6)
    return {
        "inverse": centred(key_of[0], (ORDER, ORDER), 1.0, 6.0, ((0, 4), (1, 8)), jnp.float32),
        "front_blocks": draw_front_blocks(jax.random.fold_in(key_of[5], 71), 0),
        "panels": centred(key_of[2], (FRONTS, MF, PC), MF ** -0.5, 0.09375, ((1, 4),), jnp.float32),
        "diag_terms": centred(key_of[3], (FRONTS, PC, PC), 1.0, 6.0, (), jnp.float32),
        "bounds": jax.vmap(lambda own: uneven(own, NSUP, PC, PC // 2, 2))(jax.random.split(key_of[4], FRONTS)).reshape((FRONTS, NSUP)).astype(jnp.int32),
    }


def reference(inverse, front_blocks, panels, diag_terms, bounds):
    block_count = ORDER // BS
    tile_grid = inverse.reshape(block_count, BS, block_count, BS)
    borders = []
    diagonals = []
    for front_index in range(2):
        front_list = front_blocks[front_index].astype(jnp.int32)
        front_inverse = jnp.take(tile_grid, front_list, axis=0)
        front_inverse = jnp.take(front_inverse, front_list, axis=2).reshape(MF, MF)
        border = -jnp.dot(front_inverse, panels[front_index], precision=lax.Precision.HIGHEST)
        node_ends = jnp.cumsum(bounds[front_index])
        columns = jnp.arange(PC, dtype=jnp.int32)
        node_ids = jnp.sum((columns[:, None] >= node_ends[None, :]).astype(jnp.int32), axis=1)
        same_node = (node_ids[:, None] == node_ids[None, :]).astype(jnp.float32)
        inner = jnp.dot(panels[front_index].T, border, precision=lax.Precision.HIGHEST)
        borders.append(border)
        diagonals.append(same_node * (diag_terms[front_index] - inner))
    return (jnp.stack(borders), jnp.stack(diagonals))
```

```python
import functools

import jax
import jax.numpy as jnp
from jax import lax
from jax.experimental import pallas as pl
from jax.experimental.pallas import tpu as pltpu
from jax.sharding import PartitionSpec as P

BS = 256
MESH = pl.DeviceIdType.MESH


def split(a):
    hi = a.astype(jnp.bfloat16)
    lo = (a - hi.astype(jnp.float32)).astype(jnp.bfloat16)
    return hi, lo


def dot(a, b):
    return jnp.dot(a, b, preferred_element_type=jnp.float32)


def fetch_kernel(dims, fb_hbm, inv, panels, tiles, wsel, fb, fb_sem, sem, wsem):
    fronts, kb, n_row, n_col, nz, nx, rg, cg, nh, hw = dims
    r = lax.axis_index("row")
    c = lax.axis_index("col")
    per_owner = kb // n_row
    nc = kb // n_col
    table = pltpu.make_async_copy(fb_hbm, fb, fb_sem)
    table.start()
    table.wait()
    copies = []
    for f in range(fronts):
        at = jnp.int32(0)
        for j in range(per_owner):
            at = jnp.where(fb[f, r * per_owner + j] // cg == c, j, at)
        for h in range(nh):
            copies.append(
                pltpu.make_async_copy(
                    panels.at[f, at, :, pl.ds(h * hw, hw)], wsel.at[f, h], wsem.at[f, h]
                )
            )
            copies[-1].start()
        cols = [jnp.int32(0)] * nc
        m = jnp.int32(0)
        rows = [jnp.int32(0)] * n_row
        for p in range(kb):
            b = fb[f, p]
            there = b // cg == c
            for k in range(nc):
                cols[k] = jnp.where(there & (m == k), b % cg, cols[k])
            m = m + there.astype(jnp.int32)
            t = p // per_owner
            rows[t] = jnp.where(b // rg == r, b % rg, rows[t])
        for t in range(n_row):
            for k in range(nc):
                copies.append(
                    pltpu.make_async_copy(
                        inv.at[
                            pl.ds(pl.multiple_of(rows[t] * BS, BS), BS),
                            pl.ds(pl.multiple_of(cols[k] * BS, BS), BS),
                        ],
                        tiles.at[f, t, :, pl.ds(k * BS, BS)],
                        sem.at[f, t, k],
                    )
                )
                copies[-1].start()
    for copy in copies:
        copy.wait()


class Mail:
    def __init__(self, send_sem, recv_sem):
        self.send_sem, self.recv_sem = send_sem, recv_sem
        self.sent = []

    def send(self, src, dst, peer):
        at = len(self.sent)
        copy = pltpu.make_async_remote_copy(
            src_ref=src,
            dst_ref=dst,
            send_sem=self.send_sem.at[at],
            recv_sem=self.recv_sem.at[at],
            device_id=peer,
            device_id_type=MESH,
        )
        copy.start()
        self.sent.append(copy)
        return copy

    def close(self):
        for copy in self.sent:
            copy.wait_send()


CUTS = 2
AHEAD = 4


def copies_of(dims):
    fronts, kb, n_row, n_col, nz, nx, rg, cg, nh, hw = dims
    gather = 2 * CUTS * (n_row // 2 - 1) + 1
    sums = n_row * (nx - 1) + (n_row - 1) + (nz - 1)
    diag = 2 * (n_row * nx - 1) + (nz - 1)
    return fronts * nh * (gather + sums + diag)


def node_ids(bounds, f, first, shape, dim):
    at = lax.broadcasted_iota(jnp.int32, shape, dim) + first
    ids = jnp.zeros(shape, jnp.int32)
    end = jnp.int32(0)
    for s in range(bounds.shape[1]):
        end = end + bounds[f, s]
        ids = ids + (at >= end).astype(jnp.int32)
    return ids


def main_kernel(
    dims, fb_hbm, bounds_hbm, tiles, wsel, panels, bsum, pkall,
    fb, bounds, th, tl, bm, wb, part, xbuf, xs, rbuf, qs, zbuf, pan, pth, ptl,
    dpk, rsb, zb, local_sem, send_sem, recv_sem,
):
    fronts, kb, n_row, n_col, nz, nx, rg, cg, nh, hw = dims
    r = lax.axis_index("row")
    c = lax.axis_index("col")
    s, z = lax.rem(c, nx), c // nx
    core, y, ny = lax.rem(r, 2), r // 2, n_row // 2
    per_owner = kb // n_row
    nc = kb // n_col
    share = BS // nx
    chunks = fronts * nh
    groups = n_row * nx
    half = dpk.shape[1] * dpk.shape[2]
    rows_each = dpk.shape[2]
    total_pieces = chunks * n_row

    def row_at(dy, dk):
        return lax.rem(y + dy, ny) * 2 + lax.rem(core + dk, 2)

    offsets = [(dy, dk) for dy in range(1, ny) for dk in range(2)] + [(0, 1), (0, 0)]
    slots = [row_at(dy, dk) for dy, dk in offsets]
    partner = row_at(0, 1)
    mine = r * nx + s
    plane = []
    for dy, dk in offsets:
        for ds in range(nx):
            if (dy, dk, ds) != (0, 0, 0):
                row, x = row_at(dy, dk), lax.rem(s + ds, nx)
                plane.append((row * nx + x, (row, z * nx + x)))
    depth = [lax.rem(z + d, nz) for d in range(1, nz)]

    small = [
        pltpu.make_async_copy(fb_hbm, fb, local_sem.at[0]),
        pltpu.make_async_copy(bounds_hbm, bounds, local_sem.at[1]),
    ]
    for copy in small:
        copy.start()
    own_rows = []
    for f in range(fronts):
        for j in range(nz):
            at = len(own_rows)
            copy = pltpu.make_async_copy(
                panels.at[f, j, pl.ds(pl.multiple_of(s * share, share), share), :],
                pan.at[f, j],
                local_sem.at[2 + at],
            )
            copy.start()
            own_rows.append(copy)

    barrier = pltpu.get_barrier_semaphore()
    peers = [peer for _, peer in plane] + [(r, to * nx + s) for to in depth]
    for peer in peers:
        pl.semaphore_signal(barrier, inc=1, device_id=peer, device_id_type=MESH)
    pl.semaphore_wait(barrier, len(peers))
    mail = Mail(send_sem, recv_sem)
    height = BS // CUTS
    line, beside, relayed = {}, {}, {}

    def w_send(i):
        f, h = divmod(i, nh)
        line[i] = []
        for cut in range(CUTS):
            rows = pl.ds(cut * height, height)
            for d in range(1, ny):
                copy = mail.send(wsel.at[f, h, rows], wb[i].at[r, rows], (row_at(d, 0), c))
                line[i].append((copy, row_at(ny - d, 0), rows))
        beside[i] = mail.send(wsel.at[f, h], wb[i].at[r], (partner, c))
        wb[i][r] = wsel[f, h]

    def w_relay(i):
        relayed[i] = []
        for copy, came, rows in line[i]:
            copy.wait_recv()
            piece = wb[i].at[came, rows]
            relayed[i].append(mail.send(piece, piece, (partner, c)))

    def w_ready(i):
        f = i // nh
        beside[i].wait_recv()
        for copy in relayed[i]:
            copy.wait_recv()
        own = [jnp.int32(0)] * nc
        m = jnp.int32(0)
        for p in range(kb):
            there = fb[f, p] // cg == c
            for k in range(nc):
                own[k] = jnp.where(there & (m == k), p // per_owner, own[k])
            m = m + there.astype(jnp.int32)
        for k in range(nc):
            hi, lo = split(wb[i][own[k]])
            bm[i, k * BS : (k + 1) * BS, :hw] = hi
            bm[i, k * BS : (k + 1) * BS, hw:] = lo

    def split_tiles(f):
        for t in range(n_row):
            hi, lo = split(tiles[f, t])
            th[f, t] = hi
            tl[f, t] = lo

    def split_panels(f):
        for j in range(nz):
            hi, lo = split(pan[f, j].T)
            pth[f, :, j * share : (j + 1) * share] = hi
            ptl[f, :, j * share : (j + 1) * share] = lo

    along_x, along_row, along_z = {}, {}, {}

    def piece_product(n):
        i, o = divmod(n, n_row)
        f = i // nh
        t = slots[o]
        both = dot(th[f, t], bm[i])
        low = dot(tl[f, t], bm[i, :, :hw])
        total = both[:, :hw] + (both[:, hw:] + low)
        for to in range(nx):
            part[i, o, to] = total[to * share : (to + 1) * share]
        for d in range(1, nx):
            to = lax.rem(s + d, nx)
            along_x[n, d] = mail.send(
                part.at[i, o, to], xbuf.at[i, o, d - 1], (r, z * nx + to)
            )

    def piece_sum(n):
        i, o = divmod(n, n_row)
        for d in range(1, nx):
            along_x[n, d].wait_recv()
        total = part[i, o, s]
        for d in range(1, nx):
            total = total + xbuf[i, o, d - 1]
        if o == n_row - 1:
            rbuf[i][r] = total
        else:
            xs[i, o] = total
            along_row[i, o] = mail.send(xs.at[i, o], rbuf[i].at[r], (slots[o], c))

    to_plane, to_depth, back = {}, {}, {}

    def z_stage(i):
        f, h = divmod(i, nh)
        for o in range(n_row - 1):
            along_row[i, o].wait_recv()
        for j in range(nz):
            qs[i, j] = rbuf[i][fb[f, r * per_owner + j] // rg]
        whole = jnp.concatenate([qs[i, j] for j in range(nz)], axis=0)
        hi, lo = split(whole)
        both = dot(pth[f], jnp.concatenate([hi, lo], axis=1))
        inner = both[:, :hw] + (both[:, hw:] + dot(ptl[f], hi))
        ids = node_ids(bounds, f, 0, (half, hw), 0)
        same = ids == node_ids(bounds, f, h * hw, (half, hw), 1)
        packed = jnp.where(same, inner[:half], inner[half:])
        for e in range(groups):
            dpk[i, e] = packed[e * rows_each : (e + 1) * rows_each]
        for at, (e, peer) in enumerate(plane):
            to_plane[i, at] = mail.send(dpk.at[i, e], rsb.at[i, at], peer)
        for d, to in enumerate(depth, 1):
            along_z[i, d] = mail.send(qs.at[i, to], zbuf.at[i, d - 1], (r, to * nx + s))

    def diag_sum(i):
        total = dpk[i, mine]
        for at in range(len(plane)):
            to_plane[i, at].wait_recv()
            total = total + rsb[i, at]
        zb[i, z] = total
        for d, to in enumerate(depth, 1):
            piece = zb.at[i, z]
            to_depth[i, d] = mail.send(piece, piece, (r, to * nx + s))

    def diag_back(i):
        for d in range(1, nz):
            to_depth[i, d].wait_recv()
        total = zb[i, 0]
        for j in range(1, nz):
            total = total + zb[i, j]
        pkall[i, mine] = total
        for at, (_, peer) in enumerate(plane):
            piece = pkall.at[i, mine]
            back[i, at] = mail.send(piece, piece, peer)

    def finish(i):
        f, h = divmod(i, nh)
        total = qs[i, z]
        for d in range(1, nz):
            along_z[i, d].wait_recv()
            total = total + zbuf[i, d - 1]
        bsum[f, :, h * hw : (h + 1) * hw] = total

    def done(i):
        for at in range(len(plane)):
            back[i, at].wait_recv()

    w_send(0)
    w_send(1)
    split_tiles(0)
    for copy in small:
        copy.wait()
    w_relay(0)
    w_ready(0)
    for n in range(AHEAD):
        piece_product(n)
    w_relay(1)
    for i in range(2, chunks):
        w_send(i)
    for copy in own_rows:
        copy.wait()
    for f in range(1, fronts):
        split_tiles(f)
    for f in range(fronts):
        split_panels(f)

    tasks = {}

    def plan(n, task, i):
        tasks.setdefault(min(n, total_pieces - 1), []).append((task, i))

    for i in range(chunks - 1):
        last = (i + 1) * n_row - 1
        plan(last + 2, z_stage, i)
        plan(last + 4, diag_sum, i)
        plan(last + 5, finish, i)
        plan(last + 6, diag_back, i)
    for n in range(total_pieces):
        piece_sum(n)
        ahead = n + AHEAD
        if ahead < total_pieces:
            if ahead % n_row == 0:
                w_ready(ahead // n_row)
            piece_product(ahead)
        if n % 2 == 1 and 2 + n // 2 < chunks:
            w_relay(2 + n // 2)
        if n < total_pieces - 1:
            for task, i in tasks.get(n, []):
                task(i)
    last = chunks - 1
    z_stage(last)
    for task, i in tasks.get(total_pieces - 1, []):
        task(i)
    diag_sum(last)
    diag_back(last)
    finish(last)
    for i in range(chunks):
        done(i)
    mail.close()


def last_kernel(bounds, bsum, pk, terms, border, diag):
    fronts, width = terms.shape[:2]
    half, hw = pk.shape[1:]
    border[...] = -bsum[...]
    for f in range(fronts):
        for h in range(width // hw):
            cols = node_ids(bounds, f, h * hw, (half, hw), 1)
            for a in range(width // half):
                same = (node_ids(bounds, f, a * half, (half, hw), 0) == cols).astype(jnp.float32)
                at = (f, pl.ds(a * half, half), pl.ds(h * hw, hw))
                diag[at] = same * (terms[at] + pk[f * (width // hw) + h])


def body(inverse, front_blocks, panels, diag_terms, bounds):
    n_row = lax.axis_size("row")
    n_col = lax.axis_size("col")
    rows_loc, cols_loc = inverse.shape
    rg = rows_loc // BS
    cg = cols_loc // BS
    fronts, kb = front_blocks.shape
    width = panels.shape[2]
    per_owner = kb // n_row
    nc = kb // n_col
    nz = per_owner
    nx = n_col // nz
    share = BS // nx
    nh = 2
    hw = width // nh
    half = width // 2
    chunks = fronts * nh
    groups = n_row * nx
    rows_each = half // groups
    dims = (fronts, kb, n_row, n_col, nz, nx, rg, cg, nh, hw)
    f32, bf16 = jnp.float32, jnp.bfloat16
    vmem = pl.BlockSpec(memory_space=pltpu.VMEM)
    smem = pl.BlockSpec(memory_space=pltpu.SMEM)
    anywhere = pl.BlockSpec(memory_space=pl.ANY)
    blocks = panels.reshape(fronts, per_owner, BS, width)

    tiles, wsel = pl.pallas_call(
        functools.partial(fetch_kernel, dims),
        out_shape=(
            jax.ShapeDtypeStruct((fronts, n_row, BS, nc * BS), f32),
            jax.ShapeDtypeStruct((fronts, nh, BS, hw), f32),
        ),
        in_specs=[anywhere, anywhere, anywhere],
        out_specs=(vmem, vmem),
        scratch_shapes=[
            pltpu.SMEM((fronts, kb), jnp.int32),
            pltpu.SemaphoreType.DMA(()),
            pltpu.SemaphoreType.DMA((fronts, n_row, nc)),
            pltpu.SemaphoreType.DMA((fronts, nh)),
        ],
        compiler_params=pltpu.CompilerParams(vmem_limit_bytes=24 << 20),
    )(front_blocks, inverse, blocks)

    count = copies_of(dims)
    V = pltpu.VMEM
    bsum, pk = pl.pallas_call(
        functools.partial(main_kernel, dims),
        out_shape=(
            jax.ShapeDtypeStruct((fronts, share, width), f32),
            jax.ShapeDtypeStruct((chunks, groups, rows_each, hw), f32),
        ),
        in_specs=[anywhere, anywhere, vmem, vmem, anywhere],
        out_specs=(vmem, vmem),
        scratch_shapes=[
            pltpu.SMEM((fronts, kb), jnp.int32),
            pltpu.SMEM(bounds.shape, jnp.int32),
            V((fronts, n_row, BS, nc * BS), bf16),
            V((fronts, n_row, BS, nc * BS), bf16),
            V((chunks, nc * BS, 2 * hw), bf16),
            [V((n_row, BS, hw), f32)] * chunks,
            V((chunks, n_row, nx, share, hw), f32),
            V((chunks, n_row, nx - 1, share, hw), f32),
            V((chunks, n_row, share, hw), f32),
            [V((n_row, share, hw), f32)] * chunks,
            V((chunks, nz, share, hw), f32),
            V((chunks, nz - 1, share, hw), f32),
            V((fronts, nz, share, width), f32),
            V((fronts, width, nz * share), bf16),
            V((fronts, width, nz * share), bf16),
            V((chunks, groups, rows_each, hw), f32),
            V((chunks, groups - 1, rows_each, hw), f32),
            V((chunks, nz, rows_each, hw), f32),
            pltpu.SemaphoreType.DMA((2 + fronts * nz,)),
            pltpu.SemaphoreType.DMA((count,)),
            pltpu.SemaphoreType.DMA((count,)),
        ],
        compiler_params=pltpu.CompilerParams(
            collective_id=0, has_side_effects=True, vmem_limit_bytes=48 << 20
        ),
    )(front_blocks, bounds, tiles, wsel, blocks)

    return pl.pallas_call(
        last_kernel,
        out_shape=(
            jax.ShapeDtypeStruct((fronts, share, width), f32),
            jax.ShapeDtypeStruct((fronts, width, width), f32),
        ),
        in_specs=[smem, vmem, vmem, vmem],
        out_specs=(vmem, vmem),
        compiler_params=pltpu.CompilerParams(vmem_limit_bytes=16 << 20),
    )(bounds, bsum, pk.reshape(chunks, half, hw), diag_terms)


def solution(mesh):
    placed = (P("row", "col"), P(), P(None, "row", None), P(), P())
    return jax.shard_map(
        body,
        mesh=mesh,
        in_specs=placed,
        out_specs=(P(None, ("row", "col"), None), P()),
        check_vma=False,
    )
```

```python
import functools

import jax
import jax.numpy as jnp
from jax import lax
from jax.experimental import pallas as pl
from jax.experimental.pallas import tpu as pltpu
from jax.sharding import PartitionSpec as P

BS = 256
MESH = pl.DeviceIdType.MESH


def split(a):
    hi = a.astype(jnp.bfloat16)
    lo = (a - hi.astype(jnp.float32)).astype(jnp.bfloat16)
    return hi, lo


def dot(a, b):
    return jnp.dot(a, b, preferred_element_type=jnp.float32)


def fetch_kernel(dims, fb_hbm, inv, tiles, fb, fb_sem, sem):
    fronts, kb, n_row, n_col, nz, nx, rg, cg, nh, hw = dims
    r = lax.axis_index("row")
    c = lax.axis_index("col")
    per_owner = kb // n_row
    nc = kb // n_col
    table = pltpu.make_async_copy(fb_hbm, fb, fb_sem)
    table.start()
    table.wait()
    copies = []
    for f in range(fronts):
        cols = [jnp.int32(0)] * nc
        m = jnp.int32(0)
        rows = [jnp.int32(0)] * n_row
        for p in range(kb):
            b = fb[f, p]
            there = b // cg == c
            for k in range(nc):
                cols[k] = jnp.where(there & (m == k), b % cg, cols[k])
            m = m + there.astype(jnp.int32)
            t = p // per_owner
            rows[t] = jnp.where(b // rg == r, b % rg, rows[t])
        for t in range(n_row):
            for k in range(nc):
                copies.append(
                    pltpu.make_async_copy(
                        inv.at[
                            pl.ds(pl.multiple_of(rows[t] * BS, BS), BS),
                            pl.ds(pl.multiple_of(cols[k] * BS, BS), BS),
                        ],
                        tiles.at[f, t, :, pl.ds(k * BS, BS)],
                        sem.at[f, t, k],
                    )
                )
                copies[-1].start()
    for copy in copies:
        copy.wait()


class Mail:
    def __init__(self, send_sem, recv_sem):
        self.send_sem, self.recv_sem = send_sem, recv_sem
        self.sent = []

    def send(self, src, dst, peer):
        at = len(self.sent)
        copy = pltpu.make_async_remote_copy(
            src_ref=src,
            dst_ref=dst,
            send_sem=self.send_sem.at[at],
            recv_sem=self.recv_sem.at[at],
            device_id=peer,
            device_id_type=MESH,
        )
        copy.start()
        self.sent.append(copy)
        return copy

    def close(self):
        for copy in self.sent:
            copy.wait_send()


CUTS = 2
AHEAD = 3


def copies_of(dims):
    fronts, kb, n_row, n_col, nz, nx, rg, cg, nh, hw = dims
    gather = 2 * CUTS * (n_row // 2 - 1) + 1
    sums = n_row * (nx - 1) + (n_row - 1) + 3
    diag = 2 * (n_row * nx - 1) + (nz - 1)
    return fronts * nh * (gather + sums + diag)


def node_ids(bounds, f, first, shape, dim):
    at = lax.broadcasted_iota(jnp.int32, shape, dim) + first
    ids = jnp.zeros(shape, jnp.int32)
    end = jnp.int32(0)
    for s in range(bounds.shape[1]):
        end = end + bounds[f, s]
        ids = ids + (at >= end).astype(jnp.int32)
    return ids


def main_kernel(
    dims, fb_hbm, bounds_hbm, tiles, panels, bsum, pkall,
    fb, bounds, th, tl, bm, wb, part, xbuf, xs, rbuf, qs, zbuf, zs, pth, ptl,
    dpk, rsb, zb, local_sem, send_sem, recv_sem,
):
    fronts, kb, n_row, n_col, nz, nx, rg, cg, nh, hw = dims
    r = lax.axis_index("row")
    c = lax.axis_index("col")
    s, z = lax.rem(c, nx), c // nx
    core, y, ny = lax.rem(r, 2), r // 2, n_row // 2
    per_owner = kb // n_row
    nc = kb // n_col
    share = BS // nx
    chunks = fronts * nh
    groups = n_row * nx
    half = dpk.shape[1] * dpk.shape[2]
    rows_each = dpk.shape[2]
    total_pieces = chunks * n_row

    def row_at(dy, dk):
        return lax.rem(y + dy, ny) * 2 + lax.rem(core + dk, 2)

    offsets = [(dy, dk) for dy in range(1, ny) for dk in range(2)] + [(0, 1), (0, 0)]
    slots = [row_at(dy, dk) for dy, dk in offsets]
    partner = row_at(0, 1)
    mine = r * nx + s
    plane = []
    for dy, dk in offsets:
        for ds in range(nx):
            if (dy, dk, ds) != (0, 0, 0):
                row, x = row_at(dy, dk), lax.rem(s + ds, nx)
                plane.append((row * nx + x, (row, z * nx + x)))
    depth = [lax.rem(z + d, nz) for d in range(1, nz)]

    small = [
        pltpu.make_async_copy(fb_hbm, fb, local_sem.at[0]),
        pltpu.make_async_copy(bounds_hbm, bounds, local_sem.at[1]),
    ]
    for copy in small:
        copy.start()
    mail = Mail(send_sem, recv_sem)
    height = BS // CUTS
    line, beside, relayed = {}, {}, {}

    def w_pick(i):
        f, h = divmod(i, nh)
        at = jnp.int32(0)
        for j in range(per_owner):
            at = jnp.where(fb[f, r * per_owner + j] // cg == c, j, at)
        wb[i][r] = panels[f, at, :, h * hw : (h + 1) * hw]

    def w_send(i):
        line[i] = []
        for cut in range(CUTS):
            rows = pl.ds(cut * height, height)
            piece = wb[i].at[r, rows]
            for d in range(1, ny):
                copy = mail.send(piece, piece, (row_at(d, 0), c))
                line[i].append((copy, row_at(ny - d, 0), rows))
        piece = wb[i].at[r]
        beside[i] = mail.send(piece, piece, (partner, c))

    def w_relay(i):
        relayed[i] = []
        for copy, came, rows in line[i]:
            copy.wait_recv()
            piece = wb[i].at[came, rows]
            relayed[i].append(mail.send(piece, piece, (partner, c)))

    def w_ready(i):
        f = i // nh
        beside[i].wait_recv()
        for copy in relayed[i]:
            copy.wait_recv()
        own = [jnp.int32(0)] * nc
        m = jnp.int32(0)
        for p in range(kb):
            there = fb[f, p] // cg == c
            for k in range(nc):
                own[k] = jnp.where(there & (m == k), p // per_owner, own[k])
            m = m + there.astype(jnp.int32)
        for k in range(nc):
            hi, lo = split(wb[i][own[k]])
            bm[i, k * BS : (k + 1) * BS, :hw] = hi
            bm[i, k * BS : (k + 1) * BS, hw:] = lo

    def split_tiles(f):
        for t in range(n_row):
            hi, lo = split(tiles[f, t])
            th[f, t] = hi
            tl[f, t] = lo

    def split_panels(f):
        for j in range(nz):
            own = panels[f, j, pl.ds(pl.multiple_of(s * share, share), share), :]
            hi, lo = split(own.T)
            pth[f, :, j * share : (j + 1) * share] = hi
            ptl[f, :, j * share : (j + 1) * share] = lo

    along_x, along_row, along_z = {}, {}, {}

    def piece_product(n):
        i, o = divmod(n, n_row)
        f = i // nh
        t = slots[o]
        both = dot(th[f, t], bm[i])
        low = dot(tl[f, t], bm[i, :, :hw])
        total = both[:, :hw] + (both[:, hw:] + low)
        for to in range(nx):
            part[i, o, to] = total[to * share : (to + 1) * share]
        for d in range(1, nx):
            to = lax.rem(s + d, nx)
            along_x[n, d] = mail.send(
                part.at[i, o, to], xbuf.at[i, o, d - 1], (r, z * nx + to)
            )

    def piece_sum(n):
        i, o = divmod(n, n_row)
        for d in range(1, nx):
            along_x[n, d].wait_recv()
        total = part[i, o, s]
        for d in range(1, nx):
            total = total + xbuf[i, o, d - 1]
        if o == n_row - 1:
            rbuf[i][r] = total
        else:
            xs[i, o] = total
            along_row[i, o] = mail.send(xs.at[i, o], rbuf[i].at[r], (slots[o], c))

    to_plane, to_depth, back = {}, {}, {}

    def z_stage(i):
        f, h = divmod(i, nh)
        for o in range(n_row - 1):
            along_row[i, o].wait_recv()
        for j in range(nz):
            qs[i, j] = rbuf[i][fb[f, r * per_owner + j] // rg]
        whole = jnp.concatenate([qs[i, j] for j in range(nz)], axis=0)
        hi, lo = split(whole)
        both = dot(pth[f], jnp.concatenate([hi, lo], axis=1))
        inner = both[:, :hw] + (both[:, hw:] + dot(ptl[f], hi))
        ids = node_ids(bounds, f, 0, (half, hw), 0)
        same = ids == node_ids(bounds, f, h * hw, (half, hw), 1)
        packed = jnp.where(same, inner[:half], inner[half:])
        for e in range(groups):
            dpk[i, e] = packed[e * rows_each : (e + 1) * rows_each]
        for at, (e, peer) in enumerate(plane):
            to_plane[i, at] = mail.send(dpk.at[i, e], rsb.at[i, at], peer)
        near = z + 1 - 2 * lax.rem(z, 2)
        for at in (1, 0):
            along_z[i, at] = mail.send(
                qs.at[i, lax.rem(near + 2 * at, nz)], zbuf.at[i, at], (r, near * nx + s)
            )

    def z_second(i):
        far = lax.rem(z + 2, nz)
        along_z[i, 1].wait_recv()
        zs[i] = qs[i, far] + zbuf[i, 1]
        along_z[i, 2] = mail.send(zs.at[i], zbuf.at[i, 2], (r, far * nx + s))

    def diag_sum(i):
        total = dpk[i, mine]
        for at in range(len(plane)):
            to_plane[i, at].wait_recv()
            total = total + rsb[i, at]
        zb[i, z] = total
        for d, to in enumerate(depth, 1):
            piece = zb.at[i, z]
            to_depth[i, d] = mail.send(piece, piece, (r, to * nx + s))

    def diag_back(i):
        for d in range(1, nz):
            to_depth[i, d].wait_recv()
        total = zb[i, 0]
        for j in range(1, nz):
            total = total + zb[i, j]
        pkall[i, mine] = total
        for at, (_, peer) in enumerate(plane):
            piece = pkall.at[i, mine]
            back[i, at] = mail.send(piece, piece, peer)

    def finish(i):
        f, h = divmod(i, nh)
        along_z[i, 0].wait_recv()
        total = qs[i, z] + zbuf[i, 0]
        along_z[i, 2].wait_recv()
        total = total + zbuf[i, 2]
        bsum[f, :, h * hw : (h + 1) * hw] = total

    def done(i):
        for at in range(len(plane)):
            back[i, at].wait_recv()

    barrier = pltpu.get_barrier_semaphore()
    peers = [peer for _, peer in plane] + [(r, to * nx + s) for to in depth]
    for peer in peers:
        pl.semaphore_signal(barrier, inc=1, device_id=peer, device_id_type=MESH)
    for copy in small:
        copy.wait()
    for i in range(chunks):
        w_pick(i)
    pl.semaphore_wait(barrier, len(peers))
    w_send(0)
    w_send(1)
    split_tiles(0)
    w_relay(0)
    w_ready(0)
    for n in range(AHEAD):
        piece_product(n)
    w_relay(1)
    w_send(2)
    for f in range(1, fronts):
        split_tiles(f)
    for f in range(fronts):
        split_panels(f)

    tasks = {}

    def plan(n, task, i):
        tasks.setdefault(min(n, total_pieces), []).append((task, i))

    for i in range(chunks - 1):
        last = (i + 1) * n_row - 1
        plan(last + 1, z_stage, i)
        plan(last + 3, diag_sum, i)
        plan(last + 4, z_second, i)
        plan(last + 5, diag_back, i)
        plan(last + 7, finish, i)
    for i in range(2, chunks):
        if i > 2:
            plan((i - 2) * n_row - 1, w_send, i)
        plan((i - 2) * n_row + 2, w_relay, i)
    for n in range(total_pieces):
        piece_sum(n)
        ahead = n + AHEAD
        if ahead < total_pieces:
            if ahead % n_row == 0:
                w_ready(ahead // n_row)
            piece_product(ahead)
        for task, i in tasks.get(n, []):
            task(i)
    last = chunks - 1
    z_stage(last)
    for task, i in tasks.get(total_pieces, []):
        task(i)
    diag_sum(last)
    z_second(last)
    diag_back(last)
    finish(last)
    for i in range(chunks):
        done(i)
    mail.close()


def last_kernel(bounds, bsum, pk, terms, border, diag):
    fronts, width = terms.shape[:2]
    half, hw = pk.shape[1:]
    border[...] = -bsum[...]
    for f in range(fronts):
        for h in range(width // hw):
            cols = node_ids(bounds, f, h * hw, (half, hw), 1)
            for a in range(width // half):
                same = (node_ids(bounds, f, a * half, (half, hw), 0) == cols).astype(jnp.float32)
                at = (f, pl.ds(a * half, half), pl.ds(h * hw, hw))
                diag[at] = same * (terms[at] + pk[f * (width // hw) + h])


def body(inverse, front_blocks, panels, diag_terms, bounds):
    n_row = lax.axis_size("row")
    n_col = lax.axis_size("col")
    rows_loc, cols_loc = inverse.shape
    rg = rows_loc // BS
    cg = cols_loc // BS
    fronts, kb = front_blocks.shape
    width = panels.shape[2]
    per_owner = kb // n_row
    nc = kb // n_col
    nz = per_owner
    nx = n_col // nz
    share = BS // nx
    nh = 2
    hw = width // nh
    half = width // 2
    chunks = fronts * nh
    groups = n_row * nx
    rows_each = half // groups
    dims = (fronts, kb, n_row, n_col, nz, nx, rg, cg, nh, hw)
    f32, bf16 = jnp.float32, jnp.bfloat16
    vmem = pl.BlockSpec(memory_space=pltpu.VMEM)
    smem = pl.BlockSpec(memory_space=pltpu.SMEM)
    anywhere = pl.BlockSpec(memory_space=pltpu.HBM)
    blocks = panels.reshape(fronts, per_owner, BS, width)

    tiles = pl.pallas_call(
        functools.partial(fetch_kernel, dims),
        out_shape=jax.ShapeDtypeStruct((fronts, n_row, BS, nc * BS), f32),
        in_specs=[anywhere, anywhere],
        out_specs=vmem,
        scratch_shapes=[
            pltpu.SMEM((fronts, kb), jnp.int32),
            pltpu.SemaphoreType.DMA(()),
            pltpu.SemaphoreType.DMA((fronts, n_row, nc)),
        ],
        compiler_params=pltpu.CompilerParams(vmem_limit_bytes=24 << 20),
    )(front_blocks, inverse)

    count = copies_of(dims)
    V = pltpu.VMEM
    bsum, pk = pl.pallas_call(
        functools.partial(main_kernel, dims),
        out_shape=(
            jax.ShapeDtypeStruct((fronts, share, width), f32),
            jax.ShapeDtypeStruct((chunks, groups, rows_each, hw), f32),
        ),
        in_specs=[anywhere, anywhere, vmem, vmem],
        out_specs=(vmem, vmem),
        scratch_shapes=[
            pltpu.SMEM((fronts, kb), jnp.int32),
            pltpu.SMEM(bounds.shape, jnp.int32),
            V((fronts, n_row, BS, nc * BS), bf16),
            V((fronts, n_row, BS, nc * BS), bf16),
            V((chunks, nc * BS, 2 * hw), bf16),
            [V((n_row, BS, hw), f32)] * chunks,
            V((chunks, n_row, nx, share, hw), f32),
            V((chunks, n_row, nx - 1, share, hw), f32),
            V((chunks, n_row, share, hw), f32),
            [V((n_row, share, hw), f32)] * chunks,
            V((chunks, nz, share, hw), f32),
            V((chunks, 3, share, hw), f32),
            V((chunks, share, hw), f32),
            V((fronts, width, nz * share), bf16),
            V((fronts, width, nz * share), bf16),
            V((chunks, groups, rows_each, hw), f32),
            V((chunks, groups - 1, rows_each, hw), f32),
            V((chunks, nz, rows_each, hw), f32),
            pltpu.SemaphoreType.DMA((2,)),
            pltpu.SemaphoreType.DMA((count,)),
            pltpu.SemaphoreType.DMA((count,)),
        ],
        compiler_params=pltpu.CompilerParams(
            collective_id=0,
            has_side_effects=True,
            vmem_limit_bytes=32 << 20,
        ),
    )(front_blocks, bounds, tiles, blocks)

    return pl.pallas_call(
        last_kernel,
        out_shape=(
            jax.ShapeDtypeStruct((fronts, share, width), f32),
            jax.ShapeDtypeStruct((fronts, width, width), f32),
        ),
        in_specs=[smem, vmem, vmem, vmem],
        out_specs=(vmem, vmem),
        compiler_params=pltpu.CompilerParams(vmem_limit_bytes=16 << 20),
    )(bounds, bsum, pk.reshape(chunks, half, hw), diag_terms)


def solution(mesh):
    placed = (P("row", "col"), P(), P(None, "row", None), P(), P())
    return jax.shard_map(
        body,
        mesh=mesh,
        in_specs=placed,
        out_specs=(P(None, ("row", "col"), None), P()),
        check_vma=False,
    )
```

```python
import functools

import jax
import jax.numpy as jnp
from jax import lax
from jax.experimental import pallas as pl
from jax.experimental.pallas import tpu as pltpu
from jax.sharding import PartitionSpec as P

BS = 256
MESH = pl.DeviceIdType.MESH


def split(a):
    hi = a.astype(jnp.bfloat16)
    lo = (a - hi.astype(jnp.float32)).astype(jnp.bfloat16)
    return hi, lo


def dot(a, b):
    return jnp.dot(a, b, preferred_element_type=jnp.float32)


def fetch_kernel(dims, fb_hbm, inv, tiles, fb, fb_sem, sem):
    fronts, kb, n_row, n_col, nz, nx, rg, cg, nh, hw = dims
    r = lax.axis_index("row")
    c = lax.axis_index("col")
    per_owner = kb // n_row
    nc = kb // n_col
    table = pltpu.make_async_copy(fb_hbm, fb, fb_sem)
    table.start()
    table.wait()
    copies = []
    for f in range(fronts):
        cols = [jnp.int32(0)] * nc
        m = jnp.int32(0)
        rows = [jnp.int32(0)] * n_row
        for p in range(kb):
            b = fb[f, p]
            there = b // cg == c
            for k in range(nc):
                cols[k] = jnp.where(there & (m == k), b % cg, cols[k])
            m = m + there.astype(jnp.int32)
            t = p // per_owner
            rows[t] = jnp.where(b // rg == r, b % rg, rows[t])
        for t in range(n_row):
            for k in range(nc):
                copies.append(
                    pltpu.make_async_copy(
                        inv.at[
                            pl.ds(pl.multiple_of(rows[t] * BS, BS), BS),
                            pl.ds(pl.multiple_of(cols[k] * BS, BS), BS),
                        ],
                        tiles.at[f, t, :, pl.ds(k * BS, BS)],
                        sem.at[f, t, k],
                    )
                )
                copies[-1].start()
    for copy in copies:
        copy.wait()


class Mail:
    def __init__(self, send_sem, recv_sem):
        self.send_sem, self.recv_sem = send_sem, recv_sem
        self.sent = []

    def send(self, src, dst, peer):
        at = len(self.sent)
        copy = pltpu.make_async_remote_copy(
            src_ref=src,
            dst_ref=dst,
            send_sem=self.send_sem.at[at],
            recv_sem=self.recv_sem.at[at],
            device_id=peer,
            device_id_type=MESH,
        )
        copy.start()
        self.sent.append(copy)
        return copy

    def close(self):
        for copy in self.sent:
            copy.wait_send()


CUTS = 2
AHEAD = 4


def copies_of(dims):
    fronts, kb, n_row, n_col, nz, nx, rg, cg, nh, hw = dims
    gather = 2 * CUTS * (n_row // 2 - 1) + 1
    sums = n_row * (nx - 1) + (n_row - 1) + 3
    diag = 2 * (n_row * nx - 1) + (nz - 1)
    return fronts * nh * (gather + sums + diag)


def node_ids(bounds, f, first, shape, dim):
    at = lax.broadcasted_iota(jnp.int32, shape, dim) + first
    ids = jnp.zeros(shape, jnp.int32)
    end = jnp.int32(0)
    for s in range(bounds.shape[1]):
        end = end + bounds[f, s]
        ids = ids + (at >= end).astype(jnp.int32)
    return ids


def main_kernel(
    dims, fb_hbm, bounds_hbm, tiles, panels, bsum, pkall,
    fb, bounds, th, tl, bm, wb, part, xbuf, xs, rbuf, qs, zbuf, zs, pth, ptl,
    dpk, csb, hs, rsb, zb, local_sem, send_sem, recv_sem,
):
    fronts, kb, n_row, n_col, nz, nx, rg, cg, nh, hw = dims
    r = lax.axis_index("row")
    c = lax.axis_index("col")
    s, z = lax.rem(c, nx), c // nx
    core, y, ny = lax.rem(r, 2), r // 2, n_row // 2
    per_owner = kb // n_row
    nc = kb // n_col
    share = BS // nx
    chunks = fronts * nh
    groups = n_row * nx
    half = dpk.shape[1] * dpk.shape[2]
    rows_each = dpk.shape[2]
    total_pieces = chunks * n_row

    def row_at(dy, dk):
        return lax.rem(y + dy, ny) * 2 + lax.rem(core + dk, 2)

    offsets = [(dy, dk) for dy in range(1, ny) for dk in range(2)] + [(0, 1), (0, 0)]
    slots = [row_at(dy, dk) for dy, dk in offsets]
    partner = row_at(0, 1)
    half_groups = ny * nx
    other = 1 - core
    flat_mine = y * nx + s
    mine = core * half_groups + flat_mine
    plane, flat = [], []
    for dy, dk in offsets:
        for ds in range(nx):
            if (dy, dk, ds) != (0, 0, 0):
                row, x = row_at(dy, dk), lax.rem(s + ds, nx)
                e = lax.rem(y + dy, ny) * nx + x
                peer = (row, z * nx + x)
                plane.append((lax.rem(core + dk, 2) * half_groups + e, peer))
                if dk == 0:
                    flat.append((e, peer))
    depth = [lax.rem(z + d, nz) for d in range(1, nz)]

    small = [
        pltpu.make_async_copy(fb_hbm, fb, local_sem.at[0]),
        pltpu.make_async_copy(bounds_hbm, bounds, local_sem.at[1]),
    ]
    for copy in small:
        copy.start()
    mail = Mail(send_sem, recv_sem)
    height = BS // CUTS
    line, beside, relayed = {}, {}, {}

    def w_pick(i):
        f, h = divmod(i, nh)
        at = jnp.int32(0)
        for j in range(per_owner):
            at = jnp.where(fb[f, r * per_owner + j] // cg == c, j, at)
        wb[i][r] = panels[f, at, :, h * hw : (h + 1) * hw]

    def w_send(i):
        line[i] = []
        for cut in range(CUTS):
            rows = pl.ds(cut * height, height)
            piece = wb[i].at[r, rows]
            for d in range(1, ny):
                copy = mail.send(piece, piece, (row_at(d, 0), c))
                line[i].append((copy, row_at(ny - d, 0), rows))
        piece = wb[i].at[r]
        beside[i] = mail.send(piece, piece, (partner, c))

    def w_relay(i):
        relayed[i] = []
        for copy, came, rows in line[i]:
            copy.wait_recv()
            piece = wb[i].at[came, rows]
            relayed[i].append(mail.send(piece, piece, (partner, c)))

    def w_ready(i):
        f = i // nh
        beside[i].wait_recv()
        for copy in relayed[i]:
            copy.wait_recv()
        own = [jnp.int32(0)] * nc
        m = jnp.int32(0)
        for p in range(kb):
            there = fb[f, p] // cg == c
            for k in range(nc):
                own[k] = jnp.where(there & (m == k), p // per_owner, own[k])
            m = m + there.astype(jnp.int32)
        for k in range(nc):
            hi, lo = split(wb[i][own[k]])
            bm[i, k * BS : (k + 1) * BS, :hw] = hi
            bm[i, k * BS : (k + 1) * BS, hw:] = lo

    def split_tiles(f):
        for t in range(n_row):
            hi, lo = split(tiles[f, t])
            th[f, t] = hi
            tl[f, t] = lo

    def split_panels(f):
        for j in range(nz):
            own = panels[f, j, pl.ds(pl.multiple_of(s * share, share), share), :]
            hi, lo = split(own.T)
            pth[f, :, j * share : (j + 1) * share] = hi
            ptl[f, :, j * share : (j + 1) * share] = lo

    along_x, along_row, along_z = {}, {}, {}

    def piece_product(n):
        i, o = divmod(n, n_row)
        f = i // nh
        t = slots[o]
        both = dot(th[f, t], bm[i])
        low = dot(tl[f, t], bm[i, :, :hw])
        total = both[:, :hw] + (both[:, hw:] + low)
        for to in range(nx):
            part[i, o, to] = total[to * share : (to + 1) * share]
        for d in range(1, nx):
            to = lax.rem(s + d, nx)
            along_x[n, d] = mail.send(
                part.at[i, o, to], xbuf.at[i, o, d - 1], (r, z * nx + to)
            )

    def piece_sum(n):
        i, o = divmod(n, n_row)
        for d in range(1, nx):
            along_x[n, d].wait_recv()
        total = part[i, o, s]
        for d in range(1, nx):
            total = total + xbuf[i, o, d - 1]
        if o == n_row - 1:
            rbuf[i][r] = total
        else:
            xs[i, o] = total
            along_row[i, o] = mail.send(xs.at[i, o], rbuf[i].at[r], (slots[o], c))

    to_core, to_plane, to_depth, back, to_half = {}, {}, {}, {}, {}

    def z_diag(i):
        f, h = divmod(i, nh)
        for o in range(n_row - 1):
            along_row[i, o].wait_recv()
        for j in range(nz):
            qs[i, j] = rbuf[i][fb[f, r * per_owner + j] // rg]
        whole = jnp.concatenate([qs[i, j] for j in range(nz)], axis=0)
        hi, lo = split(whole)
        both = dot(pth[f], jnp.concatenate([hi, lo], axis=1))
        inner = both[:, :hw] + (both[:, hw:] + dot(ptl[f], hi))
        ids = node_ids(bounds, f, 0, (half, hw), 0)
        same = ids == node_ids(bounds, f, h * hw, (half, hw), 1)
        packed = jnp.where(same, inner[:half], inner[half:])
        for e in range(groups):
            dpk[i, e] = packed[e * rows_each : (e + 1) * rows_each]
        if i == chunks - 1:
            for at, (e, peer) in enumerate(plane):
                to_plane[i, at] = mail.send(dpk.at[i, e], rsb.at[i, at], peer)
        else:
            to_core[i] = mail.send(
                dpk.at[i, pl.ds(other * half_groups, half_groups)], csb.at[i], (partner, c)
            )

    def z_first(i, slots_sent=(1, 0)):
        near = z + 1 - 2 * lax.rem(z, 2)
        for at in slots_sent:
            along_z[i, at] = mail.send(
                qs.at[i, lax.rem(near + 2 * at, nz)], zbuf.at[i, at], (r, near * nx + s)
            )

    def z_second(i):
        far = lax.rem(z + 2, nz)
        along_z[i, 1].wait_recv()
        zs[i] = qs[i, far] + zbuf[i, 1]
        along_z[i, 2] = mail.send(zs.at[i], zbuf.at[i, 2], (r, far * nx + s))

    def diag_half(i):
        to_core[i].wait_recv()
        hs[i] = dpk[i, pl.ds(core * half_groups, half_groups)] + csb[i]
        for at, (e, peer) in enumerate(flat):
            to_plane[i, at] = mail.send(hs.at[i, e], rsb.at[i, at], peer)

    def diag_sum(i):
        if i == chunks - 1:
            total, count = dpk[i, mine], len(plane)
        else:
            total, count = hs[i, flat_mine], len(flat)
        for at in range(count):
            to_plane[i, at].wait_recv()
            total = total + rsb[i, at]
        zb[i, z] = total
        for d, to in enumerate(depth, 1):
            piece = zb.at[i, z]
            to_depth[i, d] = mail.send(piece, piece, (r, to * nx + s))

    def diag_back(i):
        for d in range(1, nz):
            to_depth[i, d].wait_recv()
        total = zb[i, 0]
        for j in range(1, nz):
            total = total + zb[i, j]
        pkall[i, mine] = total
        for at, (_, peer) in enumerate(plane if i == chunks - 1 else flat):
            piece = pkall.at[i, mine]
            back[i, at] = mail.send(piece, piece, peer)

    def diag_share(i):
        for at in range(len(flat)):
            back[i, at].wait_recv()
        piece = pkall.at[i, pl.ds(core * half_groups, half_groups)]
        to_half[i] = mail.send(piece, piece, (partner, c))

    def finish(i):
        f, h = divmod(i, nh)
        along_z[i, 0].wait_recv()
        total = qs[i, z] + zbuf[i, 0]
        along_z[i, 2].wait_recv()
        total = total + zbuf[i, 2]
        bsum[f, :, h * hw : (h + 1) * hw] = total

    def done(i):
        if i == chunks - 1:
            for at in range(len(plane)):
                back[i, at].wait_recv()
        else:
            to_half[i].wait_recv()

    barrier = pltpu.get_barrier_semaphore()
    peers = [peer for _, peer in plane] + [(r, to * nx + s) for to in depth]
    for peer in peers:
        pl.semaphore_signal(barrier, inc=1, device_id=peer, device_id_type=MESH)
    for copy in small:
        copy.wait()
    for i in range(chunks):
        w_pick(i)
    pl.semaphore_wait(barrier, len(peers))
    w_send(0)
    for f in range(fronts):
        split_tiles(f)
    for f in range(fronts):
        split_panels(f)
    w_send(1)
    w_relay(0)
    w_ready(0)
    for n in range(AHEAD):
        piece_product(n)
    w_send(2)
    w_relay(1)

    tasks = {}

    def plan(n, task, i):
        if i < chunks - 1 or task in (w_send, w_relay):
            tasks.setdefault(min(n, total_pieces), []).append((task, i))

    for i in range(2, chunks):
        if i > 2:
            plan((i - 2) * n_row - 1, w_send, i)
        plan((i - 2) * n_row + 2, w_relay, i)
    for i in range(chunks):
        last = (i + 1) * n_row - 1
        plan(last + 2, diag_half, i)
        plan(last + 4, z_second, i)
        plan(last + 7, diag_sum, i)
        plan(last + 9, finish, i)
        plan(last + 11, diag_back, i)
        plan(last + 14, diag_share, i)
    for n in range(total_pieces):
        piece_sum(n)
        if n >= n_row and n % n_row == 0:
            z_diag(n // n_row - 1)
            z_first(n // n_row - 1)
        ahead = n + AHEAD
        if ahead < total_pieces:
            if ahead % n_row == 0:
                w_ready(ahead // n_row)
            piece_product(ahead)
        for task, i in tasks.get(n, []):
            task(i)
    last = chunks - 1
    late = tasks.get(total_pieces, [])

    def run(i, *wanted):
        for task, at in late:
            if at == i and task in wanted:
                task(at)

    for i in range(last - 1):
        run(i, z_second, diag_half, diag_sum)
    run(last - 1, z_second, diag_half)
    z_diag(last)
    z_first(last, (1,))
    for i in range(last - 1):
        run(i, finish, diag_back)
    run(last - 1, diag_sum)
    z_first(last, (0,))
    diag_sum(last)
    z_second(last)
    run(last - 1, diag_back)
    for i in range(last - 1):
        run(i, diag_share)
    diag_back(last)
    run(last - 1, finish, diag_share)
    finish(last)
    for i in range(chunks):
        done(i)
    mail.close()


def last_kernel(bounds, bsum, pk, terms, border, diag):
    fronts, width = terms.shape[:2]
    half, hw = pk.shape[1:]
    border[...] = -bsum[...]
    for f in range(fronts):
        for h in range(width // hw):
            cols = node_ids(bounds, f, h * hw, (half, hw), 1)
            for a in range(width // half):
                same = (node_ids(bounds, f, a * half, (half, hw), 0) == cols).astype(jnp.float32)
                at = (f, pl.ds(a * half, half), pl.ds(h * hw, hw))
                diag[at] = same * (terms[at] + pk[f * (width // hw) + h])


def body(inverse, front_blocks, panels, diag_terms, bounds):
    n_row = lax.axis_size("row")
    n_col = lax.axis_size("col")
    rows_loc, cols_loc = inverse.shape
    rg = rows_loc // BS
    cg = cols_loc // BS
    fronts, kb = front_blocks.shape
    width = panels.shape[2]
    per_owner = kb // n_row
    nc = kb // n_col
    nz = per_owner
    nx = n_col // nz
    share = BS // nx
    nh = 2
    hw = width // nh
    half = width // 2
    chunks = fronts * nh
    groups = n_row * nx
    rows_each = half // groups
    dims = (fronts, kb, n_row, n_col, nz, nx, rg, cg, nh, hw)
    f32, bf16 = jnp.float32, jnp.bfloat16
    vmem = pl.BlockSpec(memory_space=pltpu.VMEM)
    smem = pl.BlockSpec(memory_space=pltpu.SMEM)
    anywhere = pl.BlockSpec(memory_space=pltpu.HBM)
    blocks = panels.reshape(fronts, per_owner, BS, width)

    tiles = pl.pallas_call(
        functools.partial(fetch_kernel, dims),
        out_shape=jax.ShapeDtypeStruct((fronts, n_row, BS, nc * BS), f32),
        in_specs=[anywhere, anywhere],
        out_specs=vmem,
        scratch_shapes=[
            pltpu.SMEM((fronts, kb), jnp.int32),
            pltpu.SemaphoreType.DMA(()),
            pltpu.SemaphoreType.DMA((fronts, n_row, nc)),
        ],
        compiler_params=pltpu.CompilerParams(vmem_limit_bytes=24 << 20),
    )(front_blocks, inverse)

    count = copies_of(dims)
    V = pltpu.VMEM
    bsum, pk = pl.pallas_call(
        functools.partial(main_kernel, dims),
        out_shape=(
            jax.ShapeDtypeStruct((fronts, share, width), f32),
            jax.ShapeDtypeStruct((chunks, groups, rows_each, hw), f32),
        ),
        in_specs=[anywhere, anywhere, vmem, vmem],
        out_specs=(vmem, vmem),
        scratch_shapes=[
            pltpu.SMEM((fronts, kb), jnp.int32),
            pltpu.SMEM(bounds.shape, jnp.int32),
            V((fronts, n_row, BS, nc * BS), bf16),
            V((fronts, n_row, BS, nc * BS), bf16),
            V((chunks, nc * BS, 2 * hw), bf16),
            [V((n_row, BS, hw), f32)] * chunks,
            V((chunks, n_row, nx, share, hw), f32),
            V((chunks, n_row, nx - 1, share, hw), f32),
            V((chunks, n_row, share, hw), f32),
            [V((n_row, share, hw), f32)] * chunks,
            V((chunks, nz, share, hw), f32),
            V((chunks, 3, share, hw), f32),
            V((chunks, share, hw), f32),
            V((fronts, width, nz * share), bf16),
            V((fronts, width, nz * share), bf16),
            V((chunks, groups, rows_each, hw), f32),
            V((chunks, groups // 2, rows_each, hw), f32),
            V((chunks, groups // 2, rows_each, hw), f32),
            V((chunks, groups - 1, rows_each, hw), f32),
            V((chunks, nz, rows_each, hw), f32),
            pltpu.SemaphoreType.DMA((2,)),
            pltpu.SemaphoreType.DMA((count,)),
            pltpu.SemaphoreType.DMA((count,)),
        ],
        compiler_params=pltpu.CompilerParams(
            collective_id=0,
            has_side_effects=True,
            vmem_limit_bytes=32 << 20,
        ),
    )(front_blocks, bounds, tiles, blocks)

    return pl.pallas_call(
        last_kernel,
        out_shape=(
            jax.ShapeDtypeStruct((fronts, share, width), f32),
            jax.ShapeDtypeStruct((fronts, width, width), f32),
        ),
        in_specs=[smem, vmem, vmem, vmem],
        out_specs=(vmem, vmem),
        compiler_params=pltpu.CompilerParams(vmem_limit_bytes=16 << 20),
    )(bounds, bsum, pk.reshape(chunks, half, hw), diag_terms)


def solution(mesh):
    placed = (P("row", "col"), P(), P(None, "row", None), P(), P())
    return jax.shard_map(
        body,
        mesh=mesh,
        in_specs=placed,
        out_specs=(P(None, ("row", "col"), None), P()),
        check_vma=False,
    )
```

```python
import functools

import jax
import jax.numpy as jnp
from jax import lax
from jax.experimental import pallas as pl
from jax.experimental.pallas import tpu as pltpu
from jax.sharding import PartitionSpec as P

BS = 256
MESH = pl.DeviceIdType.MESH


def split(a):
    hi = a.astype(jnp.bfloat16)
    lo = (a - hi.astype(jnp.float32)).astype(jnp.bfloat16)
    return hi, lo


def dot(a, b):
    return jnp.dot(a, b, preferred_element_type=jnp.float32)


def fetch_kernel(dims, fb_hbm, inv, tiles, fb, fb_sem, sem):
    fronts, kb, n_row, n_col, nz, nx, rg, cg, nh, hw = dims
    r = lax.axis_index("row")
    c = lax.axis_index("col")
    per_owner = kb // n_row
    nc = kb // n_col
    table = pltpu.make_async_copy(fb_hbm, fb, fb_sem)
    table.start()
    table.wait()
    copies = []
    for f in range(fronts):
        cols = [jnp.int32(0)] * nc
        m = jnp.int32(0)
        rows = [jnp.int32(0)] * n_row
        for p in range(kb):
            b = fb[f, p]
            there = b // cg == c
            for k in range(nc):
                cols[k] = jnp.where(there & (m == k), b % cg, cols[k])
            m = m + there.astype(jnp.int32)
            t = p // per_owner
            rows[t] = jnp.where(b // rg == r, b % rg, rows[t])
        for t in range(n_row):
            for k in range(nc):
                copies.append(
                    pltpu.make_async_copy(
                        inv.at[
                            pl.ds(pl.multiple_of(rows[t] * BS, BS), BS),
                            pl.ds(pl.multiple_of(cols[k] * BS, BS), BS),
                        ],
                        tiles.at[f, t, :, pl.ds(k * BS, BS)],
                        sem.at[f, t, k],
                    )
                )
                copies[-1].start()
    for copy in copies:
        copy.wait()


class Mail:
    def __init__(self, send_sem, recv_sem):
        self.send_sem, self.recv_sem = send_sem, recv_sem
        self.sent = []

    def send(self, src, dst, peer):
        at = len(self.sent)
        copy = pltpu.make_async_remote_copy(
            src_ref=src,
            dst_ref=dst,
            send_sem=self.send_sem.at[at],
            recv_sem=self.recv_sem.at[at],
            device_id=peer,
            device_id_type=MESH,
        )
        copy.start()
        self.sent.append(copy)
        return copy

    def close(self):
        for copy in self.sent:
            copy.wait_send()


CUTS = 2
AHEAD = 4


def copies_of(dims):
    fronts, kb, n_row, n_col, nz, nx, rg, cg, nh, hw = dims
    gather = 2 * CUTS * (n_row // 2 - 1) + 1
    sums = n_row * (nx - 1) + (n_row - 1) + 3
    diag = 2 * (n_row * nx - 1) + (nz - 1)
    first = 3 + (nx - 1) + (n_row - 1) + (nz - 1)
    return fronts * nh * (gather + sums + diag) + first


def node_ids(bounds, f, first, shape, dim):
    at = lax.broadcasted_iota(jnp.int32, shape, dim) + first
    ids = jnp.zeros(shape, jnp.int32)
    end = jnp.int32(0)
    for s in range(bounds.shape[1]):
        end = end + bounds[f, s]
        ids = ids + (at >= end).astype(jnp.int32)
    return ids


def main_kernel(
    dims, fb_hbm, bounds_hbm, tiles, panels, bsum, pkall,
    fb, bounds, th, tl, bm, wb, part, xbuf, xs, rbuf, qs, zbuf, zs, pth, ptl,
    pfh, pfl, own_u, par_s, par_r, p0, zn, fs, zf, x0, x0r, rs0, rb0, q0, zc, inner0, tah, tal, tbh, tbl,
    dpk, csb, hs, rsb, zb, local_sem, send_sem, recv_sem,
):
    fronts, kb, n_row, n_col, nz, nx, rg, cg, nh, hw = dims
    r = lax.axis_index("row")
    c = lax.axis_index("col")
    s, z = lax.rem(c, nx), c // nx
    core, y, ny = lax.rem(r, 2), r // 2, n_row // 2
    per_owner = kb // n_row
    nc = kb // n_col
    share = BS // nx
    width = panels.shape[3]
    chunks = fronts * nh
    if chunks != 4 or nz != 4:
        raise ValueError(chunks, nz)
    groups = n_row * nx
    half = dpk.shape[1] * dpk.shape[2]
    rows_each = dpk.shape[2]
    last = chunks - 1
    direct = (0, last - 1, last)
    wide = (last,)
    total_pieces = chunks * n_row
    near = z + 1 - 2 * lax.rem(z, 2)
    far = lax.rem(z + 2, nz)
    sh2 = share // 2
    e0 = sh2 // nz
    kept = [sh2] + [share] * last

    def row_at(dy, dk):
        return lax.rem(y + dy, ny) * 2 + lax.rem(core + dk, 2)

    offsets = [(dy, dk) for dy in range(1, ny) for dk in range(2)] + [(0, 1), (0, 0)]
    slots = [row_at(dy, dk) for dy, dk in offsets]
    partner = row_at(0, 1)
    half_groups = ny * nx
    other = 1 - core
    flat_mine = y * nx + s
    mine = core * half_groups + flat_mine
    plane, flat = [], []
    for dy, dk in offsets:
        for ds in range(nx):
            if (dy, dk, ds) != (0, 0, 0):
                row, x = row_at(dy, dk), lax.rem(s + ds, nx)
                e = lax.rem(y + dy, ny) * nx + x
                peer = (row, z * nx + x)
                plane.append((lax.rem(core + dk, 2) * half_groups + e, peer))
                if dk == 0:
                    flat.append((e, peer))
    depth = [lax.rem(z + d, nz) for d in range(1, nz)]

    small = [
        pltpu.make_async_copy(fb_hbm, fb, local_sem.at[0]),
        pltpu.make_async_copy(bounds_hbm, bounds, local_sem.at[1]),
    ]
    for copy in small:
        copy.start()
    mail = Mail(send_sem, recv_sem)
    height = BS // CUTS
    line, beside, relayed = {}, {}, {}

    def w_pick(i):
        f, h = divmod(i, nh)
        at = jnp.int32(0)
        for j in range(per_owner):
            at = jnp.where(fb[f, r * per_owner + j] // cg == c, j, at)
        wb[i][r] = panels[f, at, :, h * hw : (h + 1) * hw]

    def w_send(i):
        line[i] = []
        for cut in range(CUTS):
            rows = pl.ds(cut * height, height)
            piece = wb[i].at[r, rows]
            for d in range(1, ny):
                copy = mail.send(piece, piece, (row_at(d, 0), c))
                line[i].append((copy, row_at(ny - d, 0), rows))
        piece = wb[i].at[r]
        beside[i] = mail.send(piece, piece, (partner, c))

    def w_relay(i):
        relayed[i] = []
        for copy, came, rows in line[i]:
            copy.wait_recv()
            piece = wb[i].at[came, rows]
            relayed[i].append(mail.send(piece, piece, (partner, c)))

    def w_ready(i):
        f = i // nh
        beside[i].wait_recv()
        for copy in relayed[i]:
            copy.wait_recv()
        own = [jnp.int32(0)] * nc
        m = jnp.int32(0)
        for p in range(kb):
            there = fb[f, p] // cg == c
            for k in range(nc):
                own[k] = jnp.where(there & (m == k), p // per_owner, own[k])
            m = m + there.astype(jnp.int32)
        for k in range(nc):
            hi, lo = split(wb[i][own[k]])
            bm[i, k * BS : (k + 1) * BS, :hw] = hi
            bm[i, k * BS : (k + 1) * BS, hw:] = lo

    def split_tiles(f):
        for t in range(n_row):
            hi, lo = split(tiles[f, t])
            th[f, t] = hi
            tl[f, t] = lo

    def split_panels(f):
        for j in range(nz):
            own = panels[f, j, pl.ds(pl.multiple_of(s * share, share), share), :]
            hi, lo = split(own.T)
            pth[f, j] = hi
            ptl[f, j] = lo
            hi, lo = split(panels[f, j].T)
            pfh[f, j] = hi
            pfl[f, j] = lo

    def split_first():
        upper = pl.ds(pl.multiple_of(s * share, share), sh2)
        lower = pl.ds(pl.multiple_of(s * share + sh2 + z * e0, e0), e0)
        for j in range(nz):
            hi, lo = split(panels[0, j, upper, :].T)
            tah[:, j * sh2 : (j + 1) * sh2] = hi
            tal[:, j * sh2 : (j + 1) * sh2] = lo
        own = jnp.concatenate([panels[0, j, lower, :] for j in range(nz)], axis=0)
        hi, lo = split(own.T)
        tbh[...] = hi
        tbl[...] = lo

    along_x, along_row, along_z = {}, {}, {}
    to_core, to_plane, to_depth, back, to_half = {}, {}, {}, {}, {}

    def x_peers():
        for d in range(1, nx):
            to = lax.rem(s + d, nx)
            yield d, to, (r, z * nx + to)

    order = [divmod(n, n_row) for n in range(total_pieces)]
    order.remove((last - 1, n_row - 1))
    order.insert(order.index((last, n_row - 2)), (last - 1, n_row - 1))

    def piece_product(n):
        i, o = order[n]
        f, keep = i // nh, kept[i]
        both = dot(th[f, slots[o]], bm[i])
        low = dot(tl[f, slots[o]], bm[i, :, :hw])
        total = both[:, :hw] + (both[:, hw:] + low)
        if i > 0 and o == n_row - 1:
            own_u[i] = total
        if i > 0 and o == n_row - 2:
            par_s[i] = total
            along_row[i, "whole"] = mail.send(par_s.at[i], par_r.at[i], (partner, c))
        for to in range(nx):
            part[i, o, to, :keep] = total[to * share : to * share + keep]
        rows = pl.ds(0, keep)
        for d, to, peer in x_peers():
            along_x[n, d] = mail.send(
                part.at[i, o, to, rows], xbuf.at[i, o, d - 1, rows], peer
            )
        if i > 0:
            return
        for x in range(nx):
            for q in range(nz):
                at = x * share + sh2 + q * e0
                p0[q, o, x] = total[at : at + e0]
        if o == n_row - 1:
            for at in (1, 0):
                along_z["near", at] = mail.send(
                    p0.at[lax.rem(near + 2 * at, nz)], zn.at[at], (r, near * nx + s)
                )

    def piece_sum(n):
        i, o = order[n]
        keep = kept[i]
        total = part[i, o, s, :keep]
        for d in range(1, nx):
            along_x[n, d].wait_recv()
            total = total + xbuf[i, o, d - 1, :keep]
        if o == n_row - 1:
            rbuf[i][r, :keep] = total
        else:
            xs[i, o, :keep] = total
            rows = pl.ds(0, keep)
            along_row[i, o] = mail.send(
                xs.at[i, o, rows], rbuf[i].at[r, rows], (slots[o], c)
            )

    def first_far():
        along_z["near", 1].wait_recv()
        fs[...] = p0[far] + zn[1]
        along_z["far"] = mail.send(fs, zf, (r, far * nx + s))

    def first_x():
        along_z["near", 0].wait_recv()
        along_z["far"].wait_recv()
        for x in range(nx):
            for o in range(n_row):
                x0[x, o] = p0[z, o, x] + zn[0, o, x] + zf[o, x]
        for d, to, peer in x_peers():
            along_x["first", d] = mail.send(x0.at[to], x0r.at[d - 1], peer)

    def first_row():
        for d in range(1, nx):
            along_x["first", d].wait_recv()
        for o in range(n_row):
            total = x0[s, o]
            for d in range(1, nx):
                total = total + x0r[d - 1, o]
            if o == n_row - 1:
                rb0[r] = total
            else:
                rs0[o] = total
                along_row["first", o] = mail.send(rs0.at[o], rb0.at[r], (slots[o], c))

    def first_join():
        for o in range(n_row - 1):
            along_row["first", o].wait_recv()
        for j in range(nz):
            q0[j] = rb0[fb[0, r * per_owner + j] // rg]
        whole = jnp.concatenate([q0[j] for j in range(nz)], axis=0)
        diag_start(0, inner_product(whole, tbh, tbl) + inner0[...])
        zc[z] = q0[z]
        for d, to in enumerate(depth, 1):
            along_z["owner", d] = mail.send(q0.at[to], zc.at[z], (r, to * nx + s))

    def first_finish():
        for d in range(1, nz):
            along_z["owner", d].wait_recv()
        for q in range(nz):
            bsum[0, sh2 + q * e0 : sh2 + (q + 1) * e0, :hw] = zc[q]

    def inner_product(whole, left_hi, left_lo):
        hi, lo = split(whole)
        both = dot(left_hi[...], jnp.concatenate([hi, lo], axis=1))
        return both[:, :hw] + (both[:, hw:] + dot(left_lo[...], hi))

    def diag_start(i, inner):
        f, h = divmod(i, nh)
        ids = node_ids(bounds, f, 0, (half, hw), 0)
        same = ids == node_ids(bounds, f, h * hw, (half, hw), 1)
        packed = jnp.where(same, inner[:half], inner[half:])
        for e in range(groups):
            dpk[i, e] = packed[e * rows_each : (e + 1) * rows_each]
        if i in direct:
            for at, (e, peer) in enumerate(plane):
                to_plane[i, at] = mail.send(dpk.at[i, e], rsb.at[i, at], peer)
        else:
            to_core[i] = mail.send(
                dpk.at[i, pl.ds(other * half_groups, half_groups)], csb.at[i], (partner, c)
            )

    arrived = set()

    def row_wait(i, o):
        if (i, o) not in arrived:
            arrived.add((i, o))
            along_row[i, o].wait_recv()

    def position(f, g):
        at = jnp.int32(0)
        found = jnp.int32(0)
        for j in range(nz):
            hit = fb[f, r * per_owner + j] // rg == g
            at = jnp.where(hit, j, at)
            found = jnp.where(hit, 1, found)
        return at, found

    def diag_go(i):
        f = i // nh
        inner = jnp.zeros((width, hw), jnp.float32)
        along_row[i, "whole"].wait_recv()
        sources = [(r, own_u[i], pfh, pfl), (partner, par_r[i], pfh, pfl)]
        for o in range(n_row - 2):
            row_wait(i, o)
        for o in range(n_row - 2):
            sources.append((slots[o], rbuf[i][slots[o]], pth, ptl))
        for g, block, left_hi, left_lo in sources:
            j, found = position(f, g)
            if n_row != nz:
                block = jnp.where(found == 1, block, 0.0)
            inner = inner + inner_product(block, left_hi.at[f, j], left_lo.at[f, j])
        diag_start(i, inner)

    def z_diag(i):
        f, keep = i // nh, kept[i]
        for o in range(n_row - 1):
            row_wait(i, o)
        for j in range(nz):
            qs[i, j, :keep] = rbuf[i][fb[f, r * per_owner + j] // rg, :keep]
        if i == 0:
            whole = jnp.concatenate([qs[i, j, :keep] for j in range(nz)], axis=0)
            inner0[...] = inner_product(whole, tah, tal)

    def z_first(i, slots_sent=(1, 0)):
        rows = pl.ds(0, kept[i])
        for at in slots_sent:
            along_z[i, at] = mail.send(
                qs.at[i, lax.rem(near + 2 * at, nz), rows],
                zbuf.at[i, at, rows],
                (r, near * nx + s),
            )

    def z_second(i):
        keep = kept[i]
        along_z[i, 1].wait_recv()
        zs[i, :keep] = qs[i, far, :keep] + zbuf[i, 1, :keep]
        rows = pl.ds(0, keep)
        along_z[i, 2] = mail.send(zs.at[i, rows], zbuf.at[i, 2, rows], (r, far * nx + s))

    def diag_half(i):
        to_core[i].wait_recv()
        hs[i] = dpk[i, pl.ds(core * half_groups, half_groups)] + csb[i]
        for at, (e, peer) in enumerate(flat):
            to_plane[i, at] = mail.send(hs.at[i, e], rsb.at[i, at], peer)

    def diag_sum(i):
        if i in direct:
            total, count = dpk[i, mine], len(plane)
        else:
            total, count = hs[i, flat_mine], len(flat)
        for at in range(count):
            to_plane[i, at].wait_recv()
            total = total + rsb[i, at]
        zb[i, z] = total
        for d, to in enumerate(depth, 1):
            piece = zb.at[i, z]
            to_depth[i, d] = mail.send(piece, piece, (r, to * nx + s))

    def diag_back(i):
        for d in range(1, nz):
            to_depth[i, d].wait_recv()
        total = zb[i, 0]
        for j in range(1, nz):
            total = total + zb[i, j]
        pkall[i, mine] = total
        for at, (_, peer) in enumerate(plane if i in wide else flat):
            piece = pkall.at[i, mine]
            back[i, at] = mail.send(piece, piece, peer)

    def diag_share(i):
        for at in range(len(flat)):
            back[i, at].wait_recv()
        piece = pkall.at[i, pl.ds(core * half_groups, half_groups)]
        to_half[i] = mail.send(piece, piece, (partner, c))

    def finish(i):
        f, h = divmod(i, nh)
        keep = kept[i]
        along_z[i, 0].wait_recv()
        total = qs[i, z, :keep] + zbuf[i, 0, :keep]
        along_z[i, 2].wait_recv()
        bsum[f, :keep, h * hw : (h + 1) * hw] = total + zbuf[i, 2, :keep]

    def done(i):
        if i in wide:
            for at in range(len(plane)):
                back[i, at].wait_recv()
        else:
            to_half[i].wait_recv()

    barrier = pltpu.get_barrier_semaphore()
    peers = [peer for _, peer in plane] + [(r, to * nx + s) for to in depth]
    for peer in peers:
        pl.semaphore_signal(barrier, inc=1, device_id=peer, device_id_type=MESH)
    for copy in small:
        copy.wait()
    for i in range(chunks):
        w_pick(i)
    pl.semaphore_wait(barrier, len(peers))
    w_send(0)
    for f in range(fronts):
        split_tiles(f)
    for f in range(fronts):
        split_panels(f)
    w_send(1)
    w_relay(0)
    w_ready(0)
    for n in range(AHEAD):
        piece_product(n)
    w_relay(1)
    w_send(2)
    split_first()

    tasks = {}

    def plan(n, task, *args):
        tasks.setdefault(n, []).append((task, args))

    plan(n_row - 1, first_far)
    plan(n_row - 1, w_send, last)
    for i in range(last):
        end = order.index((i, n_row - 1))
        at = end + 1 if i == 0 else end
        plan(at, z_diag, i)
        plan(at, z_first, i)
        if end + 3 < total_pieces:
            plan(end + 3 + (i == 0), z_second, i)
    plan(2 * n_row - 1, diag_go, 1)
    plan(2 * n_row + 1, diag_half, 1)
    plan(max(3 * n_row - 1, order.index((2, n_row - 1)) - AHEAD), diag_go, 2)
    if 2 not in direct:
        plan(3 * n_row + 1, diag_half, 2)
    plan(total_pieces - 2, diag_go, last)
    plan(total_pieces - 3, diag_sum, 1)
    plan(3 * n_row - 2, finish, 0)
    plan(3 * n_row - 2, first_row)
    plan(total_pieces - 3, first_join)
    for n in range(total_pieces):
        piece_sum(n)
        if n == 2 * n_row - 2:
            first_x()
        ahead = n + AHEAD
        if ahead < total_pieces:
            i = order[ahead][0]
            if i > 0 and order[ahead][1] == 0:
                if i == 2:
                    w_relay(2)
                if i == last:
                    w_relay(last)
                w_ready(i)
            piece_product(ahead)
        for task, args in tasks.get(n, []):
            task(*args)
    z_diag(last)
    if order.index((2, n_row - 1)) + 3 >= total_pieces:
        z_second(last - 1)
    diag_sum(2)
    diag_sum(0)
    z_first(last, (1,))
    diag_sum(last)
    diag_back(1)
    z_second(last)
    z_first(last, (0,))
    diag_back(2)
    diag_back(0)
    diag_share(1)
    diag_back(last)
    diag_share(2)
    diag_share(0)
    finish(1)
    finish(2)
    first_finish()
    finish(last)
    for i in range(chunks):
        done(i)
    mail.close()


def last_kernel(bounds, bsum, pk, terms, border, diag):
    fronts, width = terms.shape[:2]
    half, hw = pk.shape[1:]
    border[...] = -bsum[...]
    for f in range(fronts):
        for h in range(width // hw):
            cols = node_ids(bounds, f, h * hw, (half, hw), 1)
            for a in range(width // half):
                same = (node_ids(bounds, f, a * half, (half, hw), 0) == cols).astype(jnp.float32)
                at = (f, pl.ds(a * half, half), pl.ds(h * hw, hw))
                diag[at] = same * (terms[at] + pk[f * (width // hw) + h])


def body(inverse, front_blocks, panels, diag_terms, bounds):
    n_row = lax.axis_size("row")
    n_col = lax.axis_size("col")
    rows_loc, cols_loc = inverse.shape
    rg = rows_loc // BS
    cg = cols_loc // BS
    fronts, kb = front_blocks.shape
    width = panels.shape[2]
    per_owner = kb // n_row
    nc = kb // n_col
    nz = per_owner
    nx = n_col // nz
    share = BS // nx
    nh = 2
    hw = width // nh
    half = width // 2
    chunks = fronts * nh
    groups = n_row * nx
    rows_each = half // groups
    sh2 = share // 2
    e0 = sh2 // nz
    dims = (fronts, kb, n_row, n_col, nz, nx, rg, cg, nh, hw)
    f32, bf16 = jnp.float32, jnp.bfloat16
    vmem = pl.BlockSpec(memory_space=pltpu.VMEM)
    smem = pl.BlockSpec(memory_space=pltpu.SMEM)
    anywhere = pl.BlockSpec(memory_space=pltpu.HBM)
    blocks = panels.reshape(fronts, per_owner, BS, width)

    tiles = pl.pallas_call(
        functools.partial(fetch_kernel, dims),
        out_shape=jax.ShapeDtypeStruct((fronts, n_row, BS, nc * BS), f32),
        in_specs=[anywhere, anywhere],
        out_specs=vmem,
        scratch_shapes=[
            pltpu.SMEM((fronts, kb), jnp.int32),
            pltpu.SemaphoreType.DMA(()),
            pltpu.SemaphoreType.DMA((fronts, n_row, nc)),
        ],
        compiler_params=pltpu.CompilerParams(vmem_limit_bytes=24 << 20),
    )(front_blocks, inverse)

    count = copies_of(dims)
    V = pltpu.VMEM
    bsum, pk = pl.pallas_call(
        functools.partial(main_kernel, dims),
        out_shape=(
            jax.ShapeDtypeStruct((fronts, share, width), f32),
            jax.ShapeDtypeStruct((chunks, groups, rows_each, hw), f32),
        ),
        in_specs=[anywhere, anywhere, vmem, vmem],
        out_specs=(vmem, vmem),
        scratch_shapes=[
            pltpu.SMEM((fronts, kb), jnp.int32),
            pltpu.SMEM(bounds.shape, jnp.int32),
            V((fronts, n_row, BS, nc * BS), bf16),
            V((fronts, n_row, BS, nc * BS), bf16),
            V((chunks, nc * BS, 2 * hw), bf16),
            [V((n_row, BS, hw), f32)] * chunks,
            V((chunks, n_row, nx, share, hw), f32),
            V((chunks, n_row, nx - 1, share, hw), f32),
            V((chunks, n_row, share, hw), f32),
            [V((n_row, share, hw), f32)] * chunks,
            V((chunks, nz, share, hw), f32),
            V((chunks, 3, share, hw), f32),
            V((chunks, share, hw), f32),
            V((fronts, nz, width, share), bf16),
            V((fronts, nz, width, share), bf16),
            V((fronts, nz, width, BS), bf16),
            V((fronts, nz, width, BS), bf16),
            V((chunks, BS, hw), f32),
            V((chunks, BS, hw), f32),
            V((chunks, BS, hw), f32),
            V((nz, n_row, nx, e0, hw), f32),
            V((2, n_row, nx, e0, hw), f32),
            V((n_row, nx, e0, hw), f32),
            V((n_row, nx, e0, hw), f32),
            V((nx, n_row, e0, hw), f32),
            V((nx - 1, n_row, e0, hw), f32),
            V((n_row, e0, hw), f32),
            V((n_row, e0, hw), f32),
            V((nz, e0, hw), f32),
            V((nz, e0, hw), f32),
            V((width, hw), f32),
            V((width, nz * sh2), bf16),
            V((width, nz * sh2), bf16),
            V((width, nz * e0), bf16),
            V((width, nz * e0), bf16),
            V((chunks, groups, rows_each, hw), f32),
            V((chunks, groups // 2, rows_each, hw), f32),
            V((chunks, groups // 2, rows_each, hw), f32),
            V((chunks, groups - 1, rows_each, hw), f32),
            V((chunks, nz, rows_each, hw), f32),
            pltpu.SemaphoreType.DMA((2,)),
            pltpu.SemaphoreType.DMA((count,)),
            pltpu.SemaphoreType.DMA((count,)),
        ],
        compiler_params=pltpu.CompilerParams(
            collective_id=0,
            has_side_effects=True,
            vmem_limit_bytes=32 << 20,
        ),
    )(front_blocks, bounds, tiles, blocks)

    return pl.pallas_call(
        last_kernel,
        out_shape=(
            jax.ShapeDtypeStruct((fronts, share, width), f32),
            jax.ShapeDtypeStruct((fronts, width, width), f32),
        ),
        in_specs=[smem, vmem, vmem, vmem],
        out_specs=(vmem, vmem),
        compiler_params=pltpu.CompilerParams(vmem_limit_bytes=16 << 20),
    )(bounds, bsum, pk.reshape(chunks, half, hw), diag_terms)


def solution(mesh):
    placed = (P("row", "col"), P(), P(None, "row", None), P(), P())
    return jax.shard_map(
        body,
        mesh=mesh,
        in_specs=placed,
        out_specs=(P(None, ("row", "col"), None), P()),
        check_vma=False,
    )
```

```python
import functools

import jax
import jax.numpy as jnp
from jax import lax
from jax.experimental import pallas as pl
from jax.experimental.pallas import tpu as pltpu
from jax.sharding import PartitionSpec as P

BS = 256
MESH = pl.DeviceIdType.MESH


def split(a):
    hi = a.astype(jnp.bfloat16)
    lo = (a - hi.astype(jnp.float32)).astype(jnp.bfloat16)
    return hi, lo


def dot(a, b):
    return jnp.dot(a, b, preferred_element_type=jnp.float32)


def fetch_kernel(dims, fb_hbm, inv, tiles, fb, fb_sem, sem):
    fronts, kb, n_row, n_col, nz, nx, rg, cg, nh, hw = dims
    r = lax.axis_index("row")
    c = lax.axis_index("col")
    per_owner = kb // n_row
    nc = kb // n_col
    table = pltpu.make_async_copy(fb_hbm, fb, fb_sem)
    table.start()
    table.wait()
    copies = []
    for f in range(fronts):
        cols = [jnp.int32(0)] * nc
        m = jnp.int32(0)
        rows = [jnp.int32(0)] * n_row
        for p in range(kb):
            b = fb[f, p]
            there = b // cg == c
            for k in range(nc):
                cols[k] = jnp.where(there & (m == k), b % cg, cols[k])
            m = m + there.astype(jnp.int32)
            t = p // per_owner
            rows[t] = jnp.where(b // rg == r, b % rg, rows[t])
        for t in range(n_row):
            for k in range(nc):
                copies.append(
                    pltpu.make_async_copy(
                        inv.at[
                            pl.ds(pl.multiple_of(rows[t] * BS, BS), BS),
                            pl.ds(pl.multiple_of(cols[k] * BS, BS), BS),
                        ],
                        tiles.at[f, t, :, pl.ds(k * BS, BS)],
                        sem.at[f, t, k],
                    )
                )
                copies[-1].start()
    for copy in copies:
        copy.wait()


class Mail:
    def __init__(self, send_sem, recv_sem):
        self.send_sem, self.recv_sem = send_sem, recv_sem
        self.sent = []

    def send(self, src, dst, peer):
        at = len(self.sent)
        copy = pltpu.make_async_remote_copy(
            src_ref=src,
            dst_ref=dst,
            send_sem=self.send_sem.at[at],
            recv_sem=self.recv_sem.at[at],
            device_id=peer,
            device_id_type=MESH,
        )
        copy.start()
        self.sent.append(copy)
        return copy

    def close(self):
        for copy in self.sent:
            copy.wait_send()


CUTS = 2
AHEAD = 4


def copies_of(dims):
    fronts, kb, n_row, n_col, nz, nx, rg, cg, nh, hw = dims
    gather = 2 * CUTS * (n_row // 2 - 1) + 1
    sums = n_row * (nx - 1) + (n_row - 1) + 3
    diag = 2 * (n_row * nx - 1) + (nz - 1)
    first = 3 + (nx - 1) + (n_row - 1) + (nz - 1)
    return fronts * nh * (gather + sums + diag) + first


def node_ids(bounds, f, first, shape, dim):
    at = lax.broadcasted_iota(jnp.int32, shape, dim) + first
    ids = jnp.zeros(shape, jnp.int32)
    end = jnp.int32(0)
    for s in range(bounds.shape[1]):
        end = end + bounds[f, s]
        ids = ids + (at >= end).astype(jnp.int32)
    return ids


def main_kernel(
    dims, fb_hbm, bounds_hbm, tiles, panels, bsum, pkall, masks,
    fb, bounds, th, tl, bm, wb, part, xbuf, xs, rbuf, qs, zbuf, zs, pth, ptl,
    pfh, pfl, own_u, par_s, par_r, p0, zn, fs, zf, x0, x0r, rs0, rb0, q0, zc, inner0, tah, tal, tbh, tbl,
    dpk, csb, hs, rsb, zb, local_sem, send_sem, recv_sem,
):
    fronts, kb, n_row, n_col, nz, nx, rg, cg, nh, hw = dims
    r = lax.axis_index("row")
    c = lax.axis_index("col")
    s, z = lax.rem(c, nx), c // nx
    core, y, ny = lax.rem(r, 2), r // 2, n_row // 2
    per_owner = kb // n_row
    nc = kb // n_col
    share = BS // nx
    width = panels.shape[3]
    chunks = fronts * nh
    if chunks != 4 or nz != 4:
        raise ValueError(chunks, nz)
    groups = n_row * nx
    half = dpk.shape[1] * dpk.shape[2]
    rows_each = dpk.shape[2]
    last = chunks - 1
    direct = (0, last - 1, last)
    wide = (last,)
    total_pieces = chunks * n_row
    near = z + 1 - 2 * lax.rem(z, 2)
    far = lax.rem(z + 2, nz)
    sh2 = share // 2
    e0 = sh2 // nz
    kept = [sh2] + [share] * last

    def row_at(dy, dk):
        return lax.rem(y + dy, ny) * 2 + lax.rem(core + dk, 2)

    offsets = [(dy, dk) for dy in range(1, ny) for dk in range(2)] + [(0, 1), (0, 0)]
    slots = [row_at(dy, dk) for dy, dk in offsets]
    partner = row_at(0, 1)
    half_groups = ny * nx
    other = 1 - core
    flat_mine = y * nx + s
    mine = core * half_groups + flat_mine
    plane, flat = [], []
    for dy, dk in offsets:
        for ds in range(nx):
            if (dy, dk, ds) != (0, 0, 0):
                row, x = row_at(dy, dk), lax.rem(s + ds, nx)
                e = lax.rem(y + dy, ny) * nx + x
                peer = (row, z * nx + x)
                plane.append((lax.rem(core + dk, 2) * half_groups + e, peer))
                if dk == 0:
                    flat.append((e, peer))
    depth = [lax.rem(z + d, nz) for d in range(1, nz)]

    small = [
        pltpu.make_async_copy(fb_hbm, fb, local_sem.at[0]),
        pltpu.make_async_copy(bounds_hbm, bounds, local_sem.at[1]),
    ]
    for copy in small:
        copy.start()
    mail = Mail(send_sem, recv_sem)
    height = BS // CUTS
    line, beside, relayed = {}, {}, {}

    def w_pick(i):
        f, h = divmod(i, nh)
        at = jnp.int32(0)
        for j in range(per_owner):
            at = jnp.where(fb[f, r * per_owner + j] // cg == c, j, at)
        wb[i][r] = panels[f, at, :, h * hw : (h + 1) * hw]

    def w_send(i):
        line[i] = []
        for cut in range(CUTS):
            rows = pl.ds(cut * height, height)
            piece = wb[i].at[r, rows]
            for d in range(1, ny):
                copy = mail.send(piece, piece, (row_at(d, 0), c))
                line[i].append((copy, row_at(ny - d, 0), rows))
        piece = wb[i].at[r]
        beside[i] = mail.send(piece, piece, (partner, c))

    def w_relay(i):
        relayed[i] = []
        for copy, came, rows in line[i]:
            copy.wait_recv()
            piece = wb[i].at[came, rows]
            relayed[i].append(mail.send(piece, piece, (partner, c)))

    def w_ready(i):
        f = i // nh
        beside[i].wait_recv()
        for copy in relayed[i]:
            copy.wait_recv()
        own = [jnp.int32(0)] * nc
        m = jnp.int32(0)
        for p in range(kb):
            there = fb[f, p] // cg == c
            for k in range(nc):
                own[k] = jnp.where(there & (m == k), p // per_owner, own[k])
            m = m + there.astype(jnp.int32)
        for k in range(nc):
            hi, lo = split(wb[i][own[k]])
            bm[i, k * BS : (k + 1) * BS, :hw] = hi
            bm[i, k * BS : (k + 1) * BS, hw:] = lo

    def split_tiles(f):
        for t in range(n_row):
            hi, lo = split(tiles[f, t])
            th[f, t] = hi
            tl[f, t] = lo

    def split_panels(f):
        for j in range(nz):
            own = panels[f, j, pl.ds(pl.multiple_of(s * share, share), share), :]
            hi, lo = split(own.T)
            pth[f, j] = hi
            ptl[f, j] = lo
            hi, lo = split(panels[f, j].T)
            pfh[f, j] = hi
            pfl[f, j] = lo

    def mask_nodes():
        for f in range(fronts):
            for h in range(nh):
                cols = node_ids(bounds, f, h * hw, (half, hw), 1)
                for a in range(width // half):
                    same = node_ids(bounds, f, a * half, (half, hw), 0) == cols
                    at = (f, pl.ds(a * half, half), pl.ds(h * hw, hw))
                    masks[at] = same.astype(jnp.float32)

    def split_first():
        upper = pl.ds(pl.multiple_of(s * share, share), sh2)
        lower = pl.ds(pl.multiple_of(s * share + sh2 + z * e0, e0), e0)
        for j in range(nz):
            hi, lo = split(panels[0, j, upper, :].T)
            tah[:, j * sh2 : (j + 1) * sh2] = hi
            tal[:, j * sh2 : (j + 1) * sh2] = lo
        own = jnp.concatenate([panels[0, j, lower, :] for j in range(nz)], axis=0)
        hi, lo = split(own.T)
        tbh[...] = hi
        tbl[...] = lo

    along_x, along_row, along_z = {}, {}, {}
    to_core, to_plane, to_depth, back, to_half = {}, {}, {}, {}, {}

    def x_peers():
        for d in range(1, nx):
            to = lax.rem(s + d, nx)
            yield d, to, (r, z * nx + to)

    order = [divmod(n, n_row) for n in range(total_pieces)]
    order.remove((last - 1, n_row - 1))
    order.insert(order.index((last, n_row - 2)), (last - 1, n_row - 1))

    def piece_product(n):
        i, o = order[n]
        f, keep = i // nh, kept[i]
        both = dot(th[f, slots[o]], bm[i])
        low = dot(tl[f, slots[o]], bm[i, :, :hw])
        total = both[:, :hw] + (both[:, hw:] + low)
        if i > 0 and o == n_row - 1:
            own_u[i] = total
        if i > 0 and o == n_row - 2:
            par_s[i] = total
            along_row[i, "whole"] = mail.send(par_s.at[i], par_r.at[i], (partner, c))
        for to in range(nx):
            part[i, o, to, :keep] = total[to * share : to * share + keep]
        rows = pl.ds(0, keep)
        for d, to, peer in x_peers():
            along_x[n, d] = mail.send(
                part.at[i, o, to, rows], xbuf.at[i, o, d - 1, rows], peer
            )
        if i > 0:
            return
        for x in range(nx):
            for q in range(nz):
                at = x * share + sh2 + q * e0
                p0[q, o, x] = total[at : at + e0]
        if o == n_row - 1:
            for at in (1, 0):
                along_z["near", at] = mail.send(
                    p0.at[lax.rem(near + 2 * at, nz)], zn.at[at], (r, near * nx + s)
                )

    def piece_sum(n):
        i, o = order[n]
        keep = kept[i]
        total = part[i, o, s, :keep]
        for d in range(1, nx):
            along_x[n, d].wait_recv()
            total = total + xbuf[i, o, d - 1, :keep]
        if o == n_row - 1:
            rbuf[i][r, :keep] = total
        else:
            xs[i, o, :keep] = total
            rows = pl.ds(0, keep)
            along_row[i, o] = mail.send(
                xs.at[i, o, rows], rbuf[i].at[r, rows], (slots[o], c)
            )

    def first_far():
        along_z["near", 1].wait_recv()
        fs[...] = p0[far] + zn[1]
        along_z["far"] = mail.send(fs, zf, (r, far * nx + s))

    def first_x():
        along_z["near", 0].wait_recv()
        along_z["far"].wait_recv()
        for x in range(nx):
            for o in range(n_row):
                x0[x, o] = p0[z, o, x] + zn[0, o, x] + zf[o, x]
        for d, to, peer in x_peers():
            along_x["first", d] = mail.send(x0.at[to], x0r.at[d - 1], peer)

    def first_row():
        for d in range(1, nx):
            along_x["first", d].wait_recv()
        for o in range(n_row):
            total = x0[s, o]
            for d in range(1, nx):
                total = total + x0r[d - 1, o]
            if o == n_row - 1:
                rb0[r] = total
            else:
                rs0[o] = total
                along_row["first", o] = mail.send(rs0.at[o], rb0.at[r], (slots[o], c))

    def first_join():
        for o in range(n_row - 1):
            along_row["first", o].wait_recv()
        for j in range(nz):
            q0[j] = rb0[fb[0, r * per_owner + j] // rg]
        whole = jnp.concatenate([q0[j] for j in range(nz)], axis=0)
        diag_start(0, inner_product(whole, tbh, tbl) + inner0[...])
        zc[z] = q0[z]
        for d, to in enumerate(depth, 1):
            along_z["owner", d] = mail.send(q0.at[to], zc.at[z], (r, to * nx + s))

    def first_finish():
        for d in range(1, nz):
            along_z["owner", d].wait_recv()
        for q in range(nz):
            bsum[0, sh2 + q * e0 : sh2 + (q + 1) * e0, :hw] = zc[q]

    def inner_product(whole, left_hi, left_lo):
        hi, lo = split(whole)
        both = dot(left_hi[...], jnp.concatenate([hi, lo], axis=1))
        return both[:, :hw] + (both[:, hw:] + dot(left_lo[...], hi))

    def diag_start(i, inner):
        f, h = divmod(i, nh)
        ids = node_ids(bounds, f, 0, (half, hw), 0)
        same = ids == node_ids(bounds, f, h * hw, (half, hw), 1)
        packed = jnp.where(same, inner[:half], inner[half:])
        for e in range(groups):
            dpk[i, e] = packed[e * rows_each : (e + 1) * rows_each]
        if i in direct:
            for at, (e, peer) in enumerate(plane):
                to_plane[i, at] = mail.send(dpk.at[i, e], rsb.at[i, at], peer)
        else:
            to_core[i] = mail.send(
                dpk.at[i, pl.ds(other * half_groups, half_groups)], csb.at[i], (partner, c)
            )

    arrived = set()

    def row_wait(i, o):
        if (i, o) not in arrived:
            arrived.add((i, o))
            along_row[i, o].wait_recv()

    def position(f, g):
        at = jnp.int32(0)
        found = jnp.int32(0)
        for j in range(nz):
            hit = fb[f, r * per_owner + j] // rg == g
            at = jnp.where(hit, j, at)
            found = jnp.where(hit, 1, found)
        return at, found

    def diag_go(i):
        f = i // nh
        inner = jnp.zeros((width, hw), jnp.float32)
        along_row[i, "whole"].wait_recv()
        sources = [(r, own_u[i], pfh, pfl), (partner, par_r[i], pfh, pfl)]
        for o in range(n_row - 2):
            row_wait(i, o)
        for o in range(n_row - 2):
            sources.append((slots[o], rbuf[i][slots[o]], pth, ptl))
        for g, block, left_hi, left_lo in sources:
            j, found = position(f, g)
            if n_row != nz:
                block = jnp.where(found == 1, block, 0.0)
            inner = inner + inner_product(block, left_hi.at[f, j], left_lo.at[f, j])
        diag_start(i, inner)

    def z_diag(i):
        f, keep = i // nh, kept[i]
        for o in range(n_row - 1):
            row_wait(i, o)
        for j in range(nz):
            qs[i, j, :keep] = rbuf[i][fb[f, r * per_owner + j] // rg, :keep]
        if i == 0:
            whole = jnp.concatenate([qs[i, j, :keep] for j in range(nz)], axis=0)
            inner0[...] = inner_product(whole, tah, tal)

    def z_first(i, slots_sent=(1, 0)):
        rows = pl.ds(0, kept[i])
        for at in slots_sent:
            along_z[i, at] = mail.send(
                qs.at[i, lax.rem(near + 2 * at, nz), rows],
                zbuf.at[i, at, rows],
                (r, near * nx + s),
            )

    def z_second(i):
        keep = kept[i]
        along_z[i, 1].wait_recv()
        zs[i, :keep] = qs[i, far, :keep] + zbuf[i, 1, :keep]
        rows = pl.ds(0, keep)
        along_z[i, 2] = mail.send(zs.at[i, rows], zbuf.at[i, 2, rows], (r, far * nx + s))

    def diag_half(i):
        to_core[i].wait_recv()
        hs[i] = dpk[i, pl.ds(core * half_groups, half_groups)] + csb[i]
        for at, (e, peer) in enumerate(flat):
            to_plane[i, at] = mail.send(hs.at[i, e], rsb.at[i, at], peer)

    def diag_sum(i):
        if i in direct:
            total, count = dpk[i, mine], len(plane)
        else:
            total, count = hs[i, flat_mine], len(flat)
        for at in range(count):
            to_plane[i, at].wait_recv()
            total = total + rsb[i, at]
        zb[i, z] = total
        for d, to in enumerate(depth, 1):
            piece = zb.at[i, z]
            to_depth[i, d] = mail.send(piece, piece, (r, to * nx + s))

    def diag_back(i):
        for d in range(1, nz):
            to_depth[i, d].wait_recv()
        total = zb[i, 0]
        for j in range(1, nz):
            total = total + zb[i, j]
        pkall[i, mine] = total
        for at, (_, peer) in enumerate(plane if i in wide else flat):
            piece = pkall.at[i, mine]
            back[i, at] = mail.send(piece, piece, peer)

    def diag_share(i):
        for at in range(len(flat)):
            back[i, at].wait_recv()
        piece = pkall.at[i, pl.ds(core * half_groups, half_groups)]
        to_half[i] = mail.send(piece, piece, (partner, c))

    def finish(i):
        f, h = divmod(i, nh)
        keep = kept[i]
        along_z[i, 0].wait_recv()
        total = qs[i, z, :keep] + zbuf[i, 0, :keep]
        along_z[i, 2].wait_recv()
        bsum[f, :keep, h * hw : (h + 1) * hw] = total + zbuf[i, 2, :keep]

    def done(i):
        if i in wide:
            for at in range(len(plane)):
                back[i, at].wait_recv()
        else:
            to_half[i].wait_recv()

    barrier = pltpu.get_barrier_semaphore()
    peers = [peer for _, peer in plane] + [(r, to * nx + s) for to in depth]
    for peer in peers:
        pl.semaphore_signal(barrier, inc=1, device_id=peer, device_id_type=MESH)
    for copy in small:
        copy.wait()
    for i in range(chunks):
        w_pick(i)
    pl.semaphore_wait(barrier, len(peers))
    w_send(0)
    for f in range(fronts):
        split_tiles(f)
    for f in range(fronts):
        split_panels(f)
    w_send(1)
    w_relay(0)
    w_ready(0)
    for n in range(AHEAD):
        piece_product(n)
    w_relay(1)
    w_send(2)
    split_first()
    mask_nodes()

    tasks = {}

    def plan(n, task, *args):
        tasks.setdefault(n, []).append((task, args))

    plan(n_row - 1, first_far)
    plan(n_row - 1, w_send, last)
    for i in range(last):
        end = order.index((i, n_row - 1))
        at = end + 1 if i == 0 else end
        plan(at, z_diag, i)
        plan(at, z_first, i)
        if end + 3 < total_pieces:
            plan(end + 3 + (i == 0), z_second, i)
    plan(2 * n_row - 1, diag_go, 1)
    plan(2 * n_row + 1, diag_half, 1)
    plan(max(3 * n_row - 1, order.index((2, n_row - 1)) - AHEAD), diag_go, 2)
    if 2 not in direct:
        plan(3 * n_row + 1, diag_half, 2)
    plan(total_pieces - 2, diag_go, last)
    plan(total_pieces - 3, diag_sum, 1)
    plan(3 * n_row - 2, finish, 0)
    plan(3 * n_row - 2, first_row)
    plan(total_pieces - 3, first_join)
    for n in range(total_pieces):
        piece_sum(n)
        if n == 2 * n_row - 2:
            first_x()
        ahead = n + AHEAD
        if ahead < total_pieces:
            i = order[ahead][0]
            if i > 0 and order[ahead][1] == 0:
                if i == 2:
                    w_relay(2)
                if i == last:
                    w_relay(last)
                w_ready(i)
            piece_product(ahead)
        for task, args in tasks.get(n, []):
            task(*args)
    z_diag(last)
    if order.index((2, n_row - 1)) + 3 >= total_pieces:
        z_second(last - 1)
    diag_sum(2)
    diag_sum(0)
    z_first(last, (1,))
    diag_sum(last)
    diag_back(1)
    z_second(last)
    z_first(last, (0,))
    diag_back(2)
    diag_back(0)
    diag_share(1)
    diag_back(last)
    diag_share(2)
    diag_share(0)
    finish(1)
    finish(2)
    first_finish()
    finish(last)
    for i in range(chunks):
        done(i)
    mail.close()


def last_kernel(masks, bsum, pk, terms, border, diag, neg, full, sem):
    fronts, width = terms.shape[:2]
    half, hw = pk.shape[1:]
    neg[...] = -bsum[...]
    copies = [pltpu.make_async_copy(neg, border, sem.at[fronts])]
    copies[0].start()
    for f in range(fronts):
        for h in range(width // hw):
            for a in range(width // half):
                at = (f, pl.ds(a * half, half), pl.ds(h * hw, hw))
                full[at] = masks[at] * (terms[at] + pk[f * (width // hw) + h])
        copies.append(pltpu.make_async_copy(full.at[f], diag.at[f], sem.at[f]))
        copies[-1].start()
    for copy in copies:
        copy.wait()


def body(inverse, front_blocks, panels, diag_terms, bounds):
    n_row = lax.axis_size("row")
    n_col = lax.axis_size("col")
    rows_loc, cols_loc = inverse.shape
    rg = rows_loc // BS
    cg = cols_loc // BS
    fronts, kb = front_blocks.shape
    width = panels.shape[2]
    per_owner = kb // n_row
    nc = kb // n_col
    nz = per_owner
    nx = n_col // nz
    share = BS // nx
    nh = 2
    hw = width // nh
    half = width // 2
    chunks = fronts * nh
    groups = n_row * nx
    rows_each = half // groups
    sh2 = share // 2
    e0 = sh2 // nz
    dims = (fronts, kb, n_row, n_col, nz, nx, rg, cg, nh, hw)
    f32, bf16 = jnp.float32, jnp.bfloat16
    vmem = pl.BlockSpec(memory_space=pltpu.VMEM)
    anywhere = pl.BlockSpec(memory_space=pltpu.HBM)
    blocks = panels.reshape(fronts, per_owner, BS, width)

    tiles = pl.pallas_call(
        functools.partial(fetch_kernel, dims),
        out_shape=jax.ShapeDtypeStruct((fronts, n_row, BS, nc * BS), f32),
        in_specs=[anywhere, anywhere],
        out_specs=vmem,
        scratch_shapes=[
            pltpu.SMEM((fronts, kb), jnp.int32),
            pltpu.SemaphoreType.DMA(()),
            pltpu.SemaphoreType.DMA((fronts, n_row, nc)),
        ],
        compiler_params=pltpu.CompilerParams(vmem_limit_bytes=24 << 20),
    )(front_blocks, inverse)

    count = copies_of(dims)
    V = pltpu.VMEM
    bsum, pk, masks = pl.pallas_call(
        functools.partial(main_kernel, dims),
        out_shape=(
            jax.ShapeDtypeStruct((fronts, share, width), f32),
            jax.ShapeDtypeStruct((chunks, groups, rows_each, hw), f32),
            jax.ShapeDtypeStruct((fronts, width, width), f32),
        ),
        in_specs=[anywhere, anywhere, vmem, vmem],
        out_specs=(vmem, vmem, vmem),
        scratch_shapes=[
            pltpu.SMEM((fronts, kb), jnp.int32),
            pltpu.SMEM(bounds.shape, jnp.int32),
            V((fronts, n_row, BS, nc * BS), bf16),
            V((fronts, n_row, BS, nc * BS), bf16),
            V((chunks, nc * BS, 2 * hw), bf16),
            [V((n_row, BS, hw), f32)] * chunks,
            V((chunks, n_row, nx, share, hw), f32),
            V((chunks, n_row, nx - 1, share, hw), f32),
            V((chunks, n_row, share, hw), f32),
            [V((n_row, share, hw), f32)] * chunks,
            V((chunks, nz, share, hw), f32),
            V((chunks, 3, share, hw), f32),
            V((chunks, share, hw), f32),
            V((fronts, nz, width, share), bf16),
            V((fronts, nz, width, share), bf16),
            V((fronts, nz, width, BS), bf16),
            V((fronts, nz, width, BS), bf16),
            V((chunks, BS, hw), f32),
            V((chunks, BS, hw), f32),
            V((chunks, BS, hw), f32),
            V((nz, n_row, nx, e0, hw), f32),
            V((2, n_row, nx, e0, hw), f32),
            V((n_row, nx, e0, hw), f32),
            V((n_row, nx, e0, hw), f32),
            V((nx, n_row, e0, hw), f32),
            V((nx - 1, n_row, e0, hw), f32),
            V((n_row, e0, hw), f32),
            V((n_row, e0, hw), f32),
            V((nz, e0, hw), f32),
            V((nz, e0, hw), f32),
            V((width, hw), f32),
            V((width, nz * sh2), bf16),
            V((width, nz * sh2), bf16),
            V((width, nz * e0), bf16),
            V((width, nz * e0), bf16),
            V((chunks, groups, rows_each, hw), f32),
            V((chunks, groups // 2, rows_each, hw), f32),
            V((chunks, groups // 2, rows_each, hw), f32),
            V((chunks, groups - 1, rows_each, hw), f32),
            V((chunks, nz, rows_each, hw), f32),
            pltpu.SemaphoreType.DMA((2,)),
            pltpu.SemaphoreType.DMA((count,)),
            pltpu.SemaphoreType.DMA((count,)),
        ],
        compiler_params=pltpu.CompilerParams(
            collective_id=0,
            has_side_effects=True,
            vmem_limit_bytes=32 << 20,
        ),
    )(front_blocks, bounds, tiles, blocks)

    return pl.pallas_call(
        last_kernel,
        out_shape=(
            jax.ShapeDtypeStruct((fronts, share, width), f32),
            jax.ShapeDtypeStruct((fronts, width, width), f32),
        ),
        in_specs=[vmem, vmem, vmem, vmem],
        out_specs=(anywhere, anywhere),
        scratch_shapes=[
            V((fronts, share, width), f32),
            V((fronts, width, width), f32),
            pltpu.SemaphoreType.DMA((fronts + 1,)),
        ],
        compiler_params=pltpu.CompilerParams(vmem_limit_bytes=16 << 20),
    )(masks, bsum, pk.reshape(chunks, half, hw), diag_terms)


def solution(mesh):
    placed = (P("row", "col"), P(), P(None, "row", None), P(), P())
    return jax.shard_map(
        body,
        mesh=mesh,
        in_specs=placed,
        out_specs=(P(None, ("row", "col"), None), P()),
        check_vma=False,
    )
```

```python
import functools

import jax
import jax.numpy as jnp
from jax import lax
from jax.experimental import pallas as pl
from jax.experimental.pallas import tpu as pltpu
from jax.sharding import PartitionSpec as P

BS = 256
MESH = pl.DeviceIdType.MESH


def split(a):
    hi = a.astype(jnp.bfloat16)
    lo = (a - hi.astype(jnp.float32)).astype(jnp.bfloat16)
    return hi, lo


def dot(a, b):
    return jnp.dot(a, b, preferred_element_type=jnp.float32)


def fetch_kernel(dims, fb_hbm, inv, tiles, fb, fb_sem, sem):
    fronts, kb, n_row, n_col, nz, nx, rg, cg, nh, hw = dims
    r = lax.axis_index("row")
    c = lax.axis_index("col")
    per_owner = kb // n_row
    nc = kb // n_col
    table = pltpu.make_async_copy(fb_hbm, fb, fb_sem)
    table.start()
    table.wait()
    copies = []
    for f in range(fronts):
        cols = [jnp.int32(0)] * nc
        m = jnp.int32(0)
        rows = [jnp.int32(0)] * n_row
        for p in range(kb):
            b = fb[f, p]
            there = b // cg == c
            for k in range(nc):
                cols[k] = jnp.where(there & (m == k), b % cg, cols[k])
            m = m + there.astype(jnp.int32)
            t = p // per_owner
            rows[t] = jnp.where(b // rg == r, b % rg, rows[t])
        for t in range(n_row):
            for k in range(nc):
                copies.append(
                    pltpu.make_async_copy(
                        inv.at[
                            pl.ds(pl.multiple_of(rows[t] * BS, BS), BS),
                            pl.ds(pl.multiple_of(cols[k] * BS, BS), BS),
                        ],
                        tiles.at[f, t, :, pl.ds(k * BS, BS)],
                        sem.at[f, t, k],
                    )
                )
                copies[-1].start()
    for copy in copies:
        copy.wait()


class Mail:
    def __init__(self, send_sem, recv_sem):
        self.send_sem, self.recv_sem = send_sem, recv_sem
        self.sent = []

    def send(self, src, dst, peer):
        at = len(self.sent)
        copy = pltpu.make_async_remote_copy(
            src_ref=src,
            dst_ref=dst,
            send_sem=self.send_sem.at[at],
            recv_sem=self.recv_sem.at[at],
            device_id=peer,
            device_id_type=MESH,
        )
        copy.start()
        self.sent.append(copy)
        return copy

    def close(self):
        for copy in self.sent:
            copy.wait_send()


CUTS = 2
AHEAD = 4


def copies_of(dims):
    fronts, kb, n_row, n_col, nz, nx, rg, cg, nh, hw = dims
    gather = 2 * CUTS * (n_row // 2 - 1) + 1
    sums = n_row * (nx - 1) + (n_row - 1) + 3
    diag = 2 * (n_row * nx - 1) + (nz - 1)
    first = 3 + (nx - 1) + (n_row - 1) + (nz - 1)
    return fronts * nh * (gather + sums + diag) + first


def node_ids(bounds, f, first, shape, dim):
    at = lax.broadcasted_iota(jnp.int32, shape, dim) + first
    ids = jnp.zeros(shape, jnp.int32)
    end = jnp.int32(0)
    for s in range(bounds.shape[1]):
        end = end + bounds[f, s]
        ids = ids + (at >= end).astype(jnp.int32)
    return ids


def main_kernel(
    dims, fb_hbm, bounds_hbm, tiles, panels, bsum, pkall, masks,
    fb, bounds, th, tl, bm, wb, part, xbuf, xs, rbuf, qs, zbuf, zs, pth, ptl,
    pfh, pfl, own_u, par_s, par_r, p0, zn, fs, zf, x0, x0r, rs0, rb0, q0, zc, inner0, tah, tal, tbh, tbl,
    dpk, csb, hs, rsb, zb, local_sem, send_sem, recv_sem,
):
    fronts, kb, n_row, n_col, nz, nx, rg, cg, nh, hw = dims
    r = lax.axis_index("row")
    c = lax.axis_index("col")
    s, z = lax.rem(c, nx), c // nx
    core, y, ny = lax.rem(r, 2), r // 2, n_row // 2
    per_owner = kb // n_row
    nc = kb // n_col
    share = BS // nx
    width = panels.shape[3]
    chunks = fronts * nh
    if chunks != 4 or nz != 4:
        raise ValueError(chunks, nz)
    groups = n_row * nx
    half = dpk.shape[1] * dpk.shape[2]
    rows_each = dpk.shape[2]
    last = chunks - 1
    direct = (0, last - 1, last)
    wide = (last,)
    total_pieces = chunks * n_row
    near = z + 1 - 2 * lax.rem(z, 2)
    far = lax.rem(z + 2, nz)
    sh2 = share // 2
    e0 = sh2 // nz
    kept = [sh2] + [share] * last

    def row_at(dy, dk):
        return lax.rem(y + dy, ny) * 2 + lax.rem(core + dk, 2)

    offsets = [(dy, dk) for dy in range(1, ny) for dk in range(2)] + [(0, 1), (0, 0)]
    slots = [row_at(dy, dk) for dy, dk in offsets]
    partner = row_at(0, 1)
    half_groups = ny * nx
    other = 1 - core
    flat_mine = y * nx + s
    mine = core * half_groups + flat_mine
    plane, flat = [], []
    for dy, dk in offsets:
        for ds in range(nx):
            if (dy, dk, ds) != (0, 0, 0):
                row, x = row_at(dy, dk), lax.rem(s + ds, nx)
                e = lax.rem(y + dy, ny) * nx + x
                peer = (row, z * nx + x)
                plane.append((lax.rem(core + dk, 2) * half_groups + e, peer))
                if dk == 0:
                    flat.append((e, peer))
    depth = [lax.rem(z + d, nz) for d in range(1, nz)]

    small = [
        pltpu.make_async_copy(fb_hbm, fb, local_sem.at[0]),
        pltpu.make_async_copy(bounds_hbm, bounds, local_sem.at[1]),
    ]
    for copy in small:
        copy.start()
    mail = Mail(send_sem, recv_sem)
    height = BS // CUTS
    line, beside, relayed = {}, {}, {}

    def w_pick(i):
        f, h = divmod(i, nh)
        at = jnp.int32(0)
        for j in range(per_owner):
            at = jnp.where(fb[f, r * per_owner + j] // cg == c, j, at)
        wb[i][r] = panels[f, at, :, h * hw : (h + 1) * hw]

    def w_send(i):
        line[i] = []
        for cut in range(CUTS):
            rows = pl.ds(cut * height, height)
            piece = wb[i].at[r, rows]
            for d in range(1, ny):
                copy = mail.send(piece, piece, (row_at(d, 0), c))
                line[i].append((copy, row_at(ny - d, 0), rows))
        piece = wb[i].at[r]
        beside[i] = mail.send(piece, piece, (partner, c))

    def w_relay(i):
        relayed[i] = []
        for copy, came, rows in line[i]:
            copy.wait_recv()
            piece = wb[i].at[came, rows]
            relayed[i].append(mail.send(piece, piece, (partner, c)))

    def w_ready(i):
        f = i // nh
        beside[i].wait_recv()
        for copy in relayed[i]:
            copy.wait_recv()
        own = [jnp.int32(0)] * nc
        m = jnp.int32(0)
        for p in range(kb):
            there = fb[f, p] // cg == c
            for k in range(nc):
                own[k] = jnp.where(there & (m == k), p // per_owner, own[k])
            m = m + there.astype(jnp.int32)
        for k in range(nc):
            hi, lo = split(wb[i][own[k]])
            bm[i, k * BS : (k + 1) * BS, :hw] = hi
            bm[i, k * BS : (k + 1) * BS, hw:] = lo

    def split_tiles(f):
        for t in range(n_row):
            hi, lo = split(tiles[f, t])
            th[f, t] = hi
            tl[f, t] = lo

    def split_panels(f):
        for j in range(nz):
            own = panels[f, j, pl.ds(pl.multiple_of(s * share, share), share), :]
            hi, lo = split(own.T)
            pth[f, j] = hi
            ptl[f, j] = lo
            hi, lo = split(panels[f, j].T)
            pfh[f, j] = hi
            pfl[f, j] = lo

    def mask_nodes():
        for f in range(fronts):
            for h in range(nh):
                cols = node_ids(bounds, f, h * hw, (half, hw), 1)
                for a in range(width // half):
                    same = node_ids(bounds, f, a * half, (half, hw), 0) == cols
                    at = (f, pl.ds(a * half, half), pl.ds(h * hw, hw))
                    masks[at] = same.astype(jnp.float32)

    def split_first():
        upper = pl.ds(pl.multiple_of(s * share, share), sh2)
        lower = pl.ds(pl.multiple_of(s * share + sh2 + z * e0, e0), e0)
        for j in range(nz):
            hi, lo = split(panels[0, j, upper, :].T)
            tah[:, j * sh2 : (j + 1) * sh2] = hi
            tal[:, j * sh2 : (j + 1) * sh2] = lo
        own = jnp.concatenate([panels[0, j, lower, :] for j in range(nz)], axis=0)
        hi, lo = split(own.T)
        tbh[...] = hi
        tbl[...] = lo

    along_x, along_row, along_z = {}, {}, {}
    to_core, to_plane, to_depth, back, to_half = {}, {}, {}, {}, {}

    def x_peers():
        for d in range(1, nx):
            to = lax.rem(s + d, nx)
            yield d, to, (r, z * nx + to)

    order = [divmod(n, n_row) for n in range(total_pieces)]
    order.remove((last - 1, n_row - 1))
    order.insert(order.index((last, n_row - 2)), (last - 1, n_row - 1))

    def piece_product(n):
        i, o = order[n]
        f, keep = i // nh, kept[i]
        both = dot(th[f, slots[o]], bm[i])
        low = dot(tl[f, slots[o]], bm[i, :, :hw])
        total = both[:, :hw] + (both[:, hw:] + low)
        if i > 0 and o == n_row - 1:
            own_u[i] = total
        if i > 0 and o == n_row - 2:
            par_s[i] = total
            along_row[i, "whole"] = mail.send(par_s.at[i], par_r.at[i], (partner, c))
        for to in range(nx):
            part[i, o, to, :keep] = total[to * share : to * share + keep]
        rows = pl.ds(0, keep)
        for d, to, peer in x_peers():
            along_x[n, d] = mail.send(
                part.at[i, o, to, rows], xbuf.at[i, o, d - 1, rows], peer
            )
        if i > 0:
            return
        for x in range(nx):
            for q in range(nz):
                at = x * share + sh2 + q * e0
                p0[q, o, x] = total[at : at + e0]
        if o == n_row - 1:
            for at in (1, 0):
                along_z["near", at] = mail.send(
                    p0.at[lax.rem(near + 2 * at, nz)], zn.at[at], (r, near * nx + s)
                )

    def piece_sum(n):
        i, o = order[n]
        keep = kept[i]
        total = part[i, o, s, :keep]
        for d in range(1, nx):
            along_x[n, d].wait_recv()
            total = total + xbuf[i, o, d - 1, :keep]
        if o == n_row - 1:
            rbuf[i][r, :keep] = total
        else:
            xs[i, o, :keep] = total
            rows = pl.ds(0, keep)
            along_row[i, o] = mail.send(
                xs.at[i, o, rows], rbuf[i].at[r, rows], (slots[o], c)
            )

    def first_far():
        along_z["near", 1].wait_recv()
        fs[...] = p0[far] + zn[1]
        along_z["far"] = mail.send(fs, zf, (r, far * nx + s))

    def first_x():
        along_z["near", 0].wait_recv()
        along_z["far"].wait_recv()
        for x in range(nx):
            for o in range(n_row):
                x0[x, o] = p0[z, o, x] + zn[0, o, x] + zf[o, x]
        for d, to, peer in x_peers():
            along_x["first", d] = mail.send(x0.at[to], x0r.at[d - 1], peer)

    def first_row():
        for d in range(1, nx):
            along_x["first", d].wait_recv()
        for o in range(n_row):
            total = x0[s, o]
            for d in range(1, nx):
                total = total + x0r[d - 1, o]
            if o == n_row - 1:
                rb0[r] = total
            else:
                rs0[o] = total
                along_row["first", o] = mail.send(rs0.at[o], rb0.at[r], (slots[o], c))

    def first_join():
        for o in range(n_row - 1):
            along_row["first", o].wait_recv()
        for j in range(nz):
            q0[j] = rb0[fb[0, r * per_owner + j] // rg]
        whole = jnp.concatenate([q0[j] for j in range(nz)], axis=0)
        diag_start(0, inner_product(whole, tbh, tbl) + inner0[...])
        zc[z] = q0[z]
        for d, to in enumerate(depth, 1):
            along_z["owner", d] = mail.send(q0.at[to], zc.at[z], (r, to * nx + s))

    def first_finish():
        for d in range(1, nz):
            along_z["owner", d].wait_recv()
        for q in range(nz):
            bsum[0, sh2 + q * e0 : sh2 + (q + 1) * e0, :hw] = zc[q]

    def inner_product(whole, left_hi, left_lo):
        hi, lo = split(whole)
        both = dot(left_hi[...], jnp.concatenate([hi, lo], axis=1))
        return both[:, :hw] + (both[:, hw:] + dot(left_lo[...], hi))

    def diag_start(i, inner):
        f, h = divmod(i, nh)
        ids = node_ids(bounds, f, 0, (half, hw), 0)
        same = ids == node_ids(bounds, f, h * hw, (half, hw), 1)
        packed = jnp.where(same, inner[:half], inner[half:])
        for e in range(groups):
            dpk[i, e] = packed[e * rows_each : (e + 1) * rows_each]
        if i in direct:
            for at, (e, peer) in enumerate(plane):
                to_plane[i, at] = mail.send(dpk.at[i, e], rsb.at[i, at], peer)
        else:
            to_core[i] = mail.send(
                dpk.at[i, pl.ds(other * half_groups, half_groups)], csb.at[i], (partner, c)
            )

    arrived = set()

    def row_wait(i, o):
        if (i, o) not in arrived:
            arrived.add((i, o))
            along_row[i, o].wait_recv()

    def position(f, g):
        at = jnp.int32(0)
        found = jnp.int32(0)
        for j in range(nz):
            hit = fb[f, r * per_owner + j] // rg == g
            at = jnp.where(hit, j, at)
            found = jnp.where(hit, 1, found)
        return at, found

    def diag_go(i):
        f = i // nh
        inner = jnp.zeros((width, hw), jnp.float32)
        along_row[i, "whole"].wait_recv()
        sources = [(r, own_u[i], pfh, pfl), (partner, par_r[i], pfh, pfl)]
        for o in range(n_row - 2):
            row_wait(i, o)
        for o in range(n_row - 2):
            sources.append((slots[o], rbuf[i][slots[o]], pth, ptl))
        for g, block, left_hi, left_lo in sources:
            j, found = position(f, g)
            if n_row != nz:
                block = jnp.where(found == 1, block, 0.0)
            inner = inner + inner_product(block, left_hi.at[f, j], left_lo.at[f, j])
        diag_start(i, inner)

    def z_diag(i):
        f, keep = i // nh, kept[i]
        for o in range(n_row - 1):
            row_wait(i, o)
        for j in range(nz):
            qs[i, j, :keep] = rbuf[i][fb[f, r * per_owner + j] // rg, :keep]
        if i == 0:
            whole = jnp.concatenate([qs[i, j, :keep] for j in range(nz)], axis=0)
            inner0[...] = inner_product(whole, tah, tal)

    def z_first(i, slots_sent=(1, 0)):
        rows = pl.ds(0, kept[i])
        for at in slots_sent:
            along_z[i, at] = mail.send(
                qs.at[i, lax.rem(near + 2 * at, nz), rows],
                zbuf.at[i, at, rows],
                (r, near * nx + s),
            )

    def z_second(i):
        keep = kept[i]
        along_z[i, 1].wait_recv()
        zs[i, :keep] = qs[i, far, :keep] + zbuf[i, 1, :keep]
        rows = pl.ds(0, keep)
        along_z[i, 2] = mail.send(zs.at[i, rows], zbuf.at[i, 2, rows], (r, far * nx + s))

    def diag_half(i):
        to_core[i].wait_recv()
        hs[i] = dpk[i, pl.ds(core * half_groups, half_groups)] + csb[i]
        for at, (e, peer) in enumerate(flat):
            to_plane[i, at] = mail.send(hs.at[i, e], rsb.at[i, at], peer)

    def diag_sum(i):
        if i in direct:
            total, count = dpk[i, mine], len(plane)
        else:
            total, count = hs[i, flat_mine], len(flat)
        for at in range(count):
            to_plane[i, at].wait_recv()
            total = total + rsb[i, at]
        zb[i, z] = total
        for d, to in enumerate(depth, 1):
            piece = zb.at[i, z]
            to_depth[i, d] = mail.send(piece, piece, (r, to * nx + s))

    def diag_back(i):
        for d in range(1, nz):
            to_depth[i, d].wait_recv()
        total = zb[i, 0]
        for j in range(1, nz):
            total = total + zb[i, j]
        pkall[i, mine] = total
        for at, (_, peer) in enumerate(plane if i in wide else flat):
            piece = pkall.at[i, mine]
            back[i, at] = mail.send(piece, piece, peer)

    def diag_share(i):
        for at in range(len(flat)):
            back[i, at].wait_recv()
        piece = pkall.at[i, pl.ds(core * half_groups, half_groups)]
        to_half[i] = mail.send(piece, piece, (partner, c))

    def finish(i):
        f, h = divmod(i, nh)
        keep = kept[i]
        along_z[i, 0].wait_recv()
        total = qs[i, z, :keep] + zbuf[i, 0, :keep]
        along_z[i, 2].wait_recv()
        bsum[f, :keep, h * hw : (h + 1) * hw] = total + zbuf[i, 2, :keep]

    def done(i):
        if i in wide:
            for at in range(len(plane)):
                back[i, at].wait_recv()
        else:
            to_half[i].wait_recv()

    barrier = pltpu.get_barrier_semaphore()
    peers = [peer for _, peer in plane] + [(r, to * nx + s) for to in depth]
    for peer in peers:
        pl.semaphore_signal(barrier, inc=1, device_id=peer, device_id_type=MESH)
    for copy in small:
        copy.wait()
    for i in range(chunks):
        w_pick(i)
    pl.semaphore_wait(barrier, len(peers))
    w_send(0)
    for f in range(fronts):
        split_tiles(f)
    for f in range(fronts):
        split_panels(f)
    w_send(1)
    w_relay(0)
    w_ready(0)
    for n in range(AHEAD):
        piece_product(n)
    w_relay(1)
    w_send(2)
    split_first()
    mask_nodes()

    tasks = {}

    def plan(n, task, *args):
        tasks.setdefault(n, []).append((task, args))

    plan(n_row - 1, first_far)
    plan(n_row - 1, w_send, last)
    for i in range(last):
        end = order.index((i, n_row - 1))
        at = end + 1 if i == 0 else end
        plan(at, z_diag, i)
        plan(at, z_first, i)
        if end + 3 < total_pieces:
            plan(end + 3 + (i == 0), z_second, i)
    plan(2 * n_row - 1, diag_go, 1)
    plan(2 * n_row + 1, diag_half, 1)
    plan(max(3 * n_row - 1, order.index((2, n_row - 1)) - AHEAD), diag_go, 2)
    if 2 not in direct:
        plan(3 * n_row + 1, diag_half, 2)
    plan(total_pieces - 2, diag_go, last)
    plan(total_pieces - 3, diag_sum, 1)
    plan(3 * n_row - 2, finish, 0)
    plan(3 * n_row - 2, first_row)
    plan(total_pieces - 3, first_join)
    for n in range(total_pieces):
        piece_sum(n)
        if n == 2 * n_row - 2:
            first_x()
        ahead = n + AHEAD
        if ahead < total_pieces:
            i = order[ahead][0]
            if i > 0 and order[ahead][1] == 0:
                if i == 2:
                    w_relay(2)
                if i == last:
                    w_relay(last)
                w_ready(i)
            piece_product(ahead)
        for task, args in tasks.get(n, []):
            task(*args)
    z_diag(last)
    if order.index((2, n_row - 1)) + 3 >= total_pieces:
        z_second(last - 1)
    diag_sum(2)
    diag_sum(0)
    z_first(last, (1,))
    diag_sum(last)
    diag_back(1)
    diag_back(2)
    diag_back(0)
    z_second(last)
    z_first(last, (0,))
    diag_share(1)
    diag_back(last)
    diag_share(2)
    diag_share(0)
    finish(1)
    finish(2)
    first_finish()
    finish(last)
    for i in range(chunks):
        done(i)
    mail.close()


def last_kernel(masks, bsum, pk, terms, border, diag, neg, full, sem):
    fronts, width = terms.shape[:2]
    half, hw = pk.shape[1:]
    neg[...] = -bsum[...]
    copies = [pltpu.make_async_copy(neg, border, sem.at[fronts])]
    copies[0].start()
    for f in range(fronts):
        for h in range(width // hw):
            for a in range(width // half):
                at = (f, pl.ds(a * half, half), pl.ds(h * hw, hw))
                full[at] = masks[at] * (terms[at] + pk[f * (width // hw) + h])
        copies.append(pltpu.make_async_copy(full.at[f], diag.at[f], sem.at[f]))
        copies[-1].start()
    for copy in copies:
        copy.wait()


def body(inverse, front_blocks, panels, diag_terms, bounds):
    n_row = lax.axis_size("row")
    n_col = lax.axis_size("col")
    rows_loc, cols_loc = inverse.shape
    rg = rows_loc // BS
    cg = cols_loc // BS
    fronts, kb = front_blocks.shape
    width = panels.shape[2]
    per_owner = kb // n_row
    nc = kb // n_col
    nz = per_owner
    nx = n_col // nz
    share = BS // nx
    nh = 2
    hw = width // nh
    half = width // 2
    chunks = fronts * nh
    groups = n_row * nx
    rows_each = half // groups
    sh2 = share // 2
    e0 = sh2 // nz
    dims = (fronts, kb, n_row, n_col, nz, nx, rg, cg, nh, hw)
    f32, bf16 = jnp.float32, jnp.bfloat16
    vmem = pl.BlockSpec(memory_space=pltpu.VMEM)
    anywhere = pl.BlockSpec(memory_space=pltpu.HBM)
    blocks = panels.reshape(fronts, per_owner, BS, width)

    tiles = pl.pallas_call(
        functools.partial(fetch_kernel, dims),
        out_shape=jax.ShapeDtypeStruct((fronts, n_row, BS, nc * BS), f32),
        in_specs=[anywhere, anywhere],
        out_specs=vmem,
        scratch_shapes=[
            pltpu.SMEM((fronts, kb), jnp.int32),
            pltpu.SemaphoreType.DMA(()),
            pltpu.SemaphoreType.DMA((fronts, n_row, nc)),
        ],
        compiler_params=pltpu.CompilerParams(vmem_limit_bytes=24 << 20),
    )(front_blocks, inverse)

    count = copies_of(dims)
    V = pltpu.VMEM
    bsum, pk, masks = pl.pallas_call(
        functools.partial(main_kernel, dims),
        out_shape=(
            jax.ShapeDtypeStruct((fronts, share, width), f32),
            jax.ShapeDtypeStruct((chunks, groups, rows_each, hw), f32),
            jax.ShapeDtypeStruct((fronts, width, width), f32),
        ),
        in_specs=[anywhere, anywhere, vmem, vmem],
        out_specs=(vmem, vmem, vmem),
        scratch_shapes=[
            pltpu.SMEM((fronts, kb), jnp.int32),
            pltpu.SMEM(bounds.shape, jnp.int32),
            V((fronts, n_row, BS, nc * BS), bf16),
            V((fronts, n_row, BS, nc * BS), bf16),
            V((chunks, nc * BS, 2 * hw), bf16),
            [V((n_row, BS, hw), f32)] * chunks,
            V((chunks, n_row, nx, share, hw), f32),
            V((chunks, n_row, nx - 1, share, hw), f32),
            V((chunks, n_row, share, hw), f32),
            [V((n_row, share, hw), f32)] * chunks,
            V((chunks, nz, share, hw), f32),
            V((chunks, 3, share, hw), f32),
            V((chunks, share, hw), f32),
            V((fronts, nz, width, share), bf16),
            V((fronts, nz, width, share), bf16),
            V((fronts, nz, width, BS), bf16),
            V((fronts, nz, width, BS), bf16),
            V((chunks, BS, hw), f32),
            V((chunks, BS, hw), f32),
            V((chunks, BS, hw), f32),
            V((nz, n_row, nx, e0, hw), f32),
            V((2, n_row, nx, e0, hw), f32),
            V((n_row, nx, e0, hw), f32),
            V((n_row, nx, e0, hw), f32),
            V((nx, n_row, e0, hw), f32),
            V((nx - 1, n_row, e0, hw), f32),
            V((n_row, e0, hw), f32),
            V((n_row, e0, hw), f32),
            V((nz, e0, hw), f32),
            V((nz, e0, hw), f32),
            V((width, hw), f32),
            V((width, nz * sh2), bf16),
            V((width, nz * sh2), bf16),
            V((width, nz * e0), bf16),
            V((width, nz * e0), bf16),
            V((chunks, groups, rows_each, hw), f32),
            V((chunks, groups // 2, rows_each, hw), f32),
            V((chunks, groups // 2, rows_each, hw), f32),
            V((chunks, groups - 1, rows_each, hw), f32),
            V((chunks, nz, rows_each, hw), f32),
            pltpu.SemaphoreType.DMA((2,)),
            pltpu.SemaphoreType.DMA((count,)),
            pltpu.SemaphoreType.DMA((count,)),
        ],
        compiler_params=pltpu.CompilerParams(
            collective_id=0,
            has_side_effects=True,
            vmem_limit_bytes=32 << 20,
        ),
    )(front_blocks, bounds, tiles, blocks)

    return pl.pallas_call(
        last_kernel,
        out_shape=(
            jax.ShapeDtypeStruct((fronts, share, width), f32),
            jax.ShapeDtypeStruct((fronts, width, width), f32),
        ),
        in_specs=[vmem, vmem, vmem, vmem],
        out_specs=(anywhere, anywhere),
        scratch_shapes=[
            V((fronts, share, width), f32),
            V((fronts, width, width), f32),
            pltpu.SemaphoreType.DMA((fronts + 1,)),
        ],
        compiler_params=pltpu.CompilerParams(vmem_limit_bytes=16 << 20),
    )(masks, bsum, pk.reshape(chunks, half, hw), diag_terms)


def solution(mesh):
    placed = (P("row", "col"), P(), P(None, "row", None), P(), P())
    return jax.shard_map(
        body,
        mesh=mesh,
        in_specs=placed,
        out_specs=(P(None, ("row", "col"), None), P()),
        check_vma=False,
    )
```

```python
import functools

import jax
import jax.numpy as jnp
from jax import lax
from jax.experimental import pallas as pl
from jax.experimental.pallas import tpu as pltpu
from jax.sharding import PartitionSpec as P

BS = 256
MESH = pl.DeviceIdType.MESH


def split(a):
    hi = a.astype(jnp.bfloat16)
    lo = (a - hi.astype(jnp.float32)).astype(jnp.bfloat16)
    return hi, lo


def dot(a, b):
    return jnp.dot(a, b, preferred_element_type=jnp.float32)


def fetch_kernel(dims, fb_hbm, inv, tiles, fb, fb_sem, sem):
    fronts, kb, n_row, n_col, nz, nx, rg, cg, nh, hw = dims
    r = lax.axis_index("row")
    c = lax.axis_index("col")
    per_owner = kb // n_row
    nc = kb // n_col
    table = pltpu.make_async_copy(fb_hbm, fb, fb_sem)
    table.start()
    table.wait()
    copies = []
    for f in range(fronts):
        cols = [jnp.int32(0)] * nc
        m = jnp.int32(0)
        for p in range(kb):
            b = fb[f, p]
            there = b // cg == c
            for k in range(nc):
                cols[k] = jnp.where(there & (m == k), b % cg, cols[k])
            m = m + there.astype(jnp.int32)
        for t in range(n_row):
            row = jnp.int32(0)
            for p in range(t * per_owner, (t + 1) * per_owner):
                b = fb[f, p]
                row = jnp.where(b // rg == r, b % rg, row)
            for k in range(nc):
                copies.append(
                    pltpu.make_async_copy(
                        inv.at[
                            pl.ds(pl.multiple_of(row * BS, BS), BS),
                            pl.ds(pl.multiple_of(cols[k] * BS, BS), BS),
                        ],
                        tiles.at[f, t, :, pl.ds(k * BS, BS)],
                        sem.at[f, t, k],
                    )
                )
                copies[-1].start()
    for copy in copies:
        copy.wait()


class Mail:
    def __init__(self, send_sem, recv_sem):
        self.send_sem, self.recv_sem = send_sem, recv_sem
        self.sent = []

    def send(self, src, dst, peer):
        at = len(self.sent)
        copy = pltpu.make_async_remote_copy(
            src_ref=src,
            dst_ref=dst,
            send_sem=self.send_sem.at[at],
            recv_sem=self.recv_sem.at[at],
            device_id=peer,
            device_id_type=MESH,
        )
        copy.start()
        self.sent.append(copy)
        return copy

    def close(self):
        for copy in self.sent:
            copy.wait_send()


CUTS = 2
AHEAD = 4


def copies_of(dims):
    fronts, kb, n_row, n_col, nz, nx, rg, cg, nh, hw = dims
    gather = 2 * CUTS * (n_row // 2 - 1) + 1
    sums = n_row * (nx - 1) + (n_row - 1) + 3
    diag = 2 * (n_row * nx - 1) + (nz - 1)
    first = 3 + (nx - 1) + (n_row - 1) + (nz - 1)
    return fronts * nh * (gather + sums + diag) + first


def node_ids(bounds, f, first, shape, dim):
    at = lax.broadcasted_iota(jnp.int32, shape, dim) + first
    ids = jnp.zeros(shape, jnp.int32)
    end = jnp.int32(0)
    for s in range(bounds.shape[1]):
        end = end + bounds[f, s]
        ids = ids + (at >= end).astype(jnp.int32)
    return ids


def main_kernel(
    dims, fb_hbm, bounds_hbm, tiles, panels, bsum, pkall, masks,
    fb, bounds, th, tl, bm, wb, part, xbuf, xs, rbuf, qs, zbuf, zs, pth, ptl,
    pfh, pfl, own_u, par_s, par_r, p0, zn, fs, zf, x0, x0r, rs0, rb0, q0, zc, inner0, tah, tal, tbh, tbl,
    dpk, csb, hs, rsb, zb, local_sem, send_sem, recv_sem,
):
    fronts, kb, n_row, n_col, nz, nx, rg, cg, nh, hw = dims
    r = lax.axis_index("row")
    c = lax.axis_index("col")
    s, z = lax.rem(c, nx), c // nx
    core, y, ny = lax.rem(r, 2), r // 2, n_row // 2
    per_owner = kb // n_row
    nc = kb // n_col
    share = BS // nx
    width = panels.shape[3]
    chunks = fronts * nh
    if chunks != 4 or nz != 4:
        raise ValueError(chunks, nz)
    groups = n_row * nx
    half = dpk.shape[1] * dpk.shape[2]
    rows_each = dpk.shape[2]
    last = chunks - 1
    direct = (0, last - 1, last)
    wide = (last,)
    total_pieces = chunks * n_row
    near = z + 1 - 2 * lax.rem(z, 2)
    far = lax.rem(z + 2, nz)
    sh2 = share // 2
    e0 = sh2 // nz
    kept = [sh2] + [share] * last

    def row_at(dy, dk):
        return lax.rem(y + dy, ny) * 2 + lax.rem(core + dk, 2)

    offsets = [(dy, dk) for dy in range(1, ny) for dk in range(2)] + [(0, 1), (0, 0)]
    slots = [row_at(dy, dk) for dy, dk in offsets]
    partner = row_at(0, 1)
    half_groups = ny * nx
    other = 1 - core
    flat_mine = y * nx + s
    mine = core * half_groups + flat_mine
    plane, flat = [], []
    for dy, dk in offsets:
        for ds in range(nx):
            if (dy, dk, ds) != (0, 0, 0):
                row, x = row_at(dy, dk), lax.rem(s + ds, nx)
                e = lax.rem(y + dy, ny) * nx + x
                peer = (row, z * nx + x)
                plane.append((lax.rem(core + dk, 2) * half_groups + e, peer))
                if dk == 0:
                    flat.append((e, peer))
    depth = [lax.rem(z + d, nz) for d in range(1, nz)]

    small = [
        pltpu.make_async_copy(fb_hbm, fb, local_sem.at[0]),
        pltpu.make_async_copy(bounds_hbm, bounds, local_sem.at[1]),
    ]
    for copy in small:
        copy.start()
    mail = Mail(send_sem, recv_sem)
    height = BS // CUTS
    line, beside, relayed = {}, {}, {}

    def w_pick(i):
        f, h = divmod(i, nh)
        at = jnp.int32(0)
        for j in range(per_owner):
            at = jnp.where(fb[f, r * per_owner + j] // cg == c, j, at)
        wb[i][r] = panels[f, at, :, h * hw : (h + 1) * hw]

    def w_send(i):
        line[i] = []
        for cut in range(CUTS):
            rows = pl.ds(cut * height, height)
            piece = wb[i].at[r, rows]
            for d in range(1, ny):
                copy = mail.send(piece, piece, (row_at(d, 0), c))
                line[i].append((copy, row_at(ny - d, 0), rows))
        piece = wb[i].at[r]
        beside[i] = mail.send(piece, piece, (partner, c))

    def w_relay(i):
        relayed[i] = []
        for copy, came, rows in line[i]:
            copy.wait_recv()
            piece = wb[i].at[came, rows]
            relayed[i].append(mail.send(piece, piece, (partner, c)))

    def w_ready(i):
        f = i // nh
        beside[i].wait_recv()
        for copy in relayed[i]:
            copy.wait_recv()
        own = [jnp.int32(0)] * nc
        m = jnp.int32(0)
        for p in range(kb):
            there = fb[f, p] // cg == c
            for k in range(nc):
                own[k] = jnp.where(there & (m == k), p // per_owner, own[k])
            m = m + there.astype(jnp.int32)
        for k in range(nc):
            hi, lo = split(wb[i][own[k]])
            bm[i, k * BS : (k + 1) * BS, :hw] = hi
            bm[i, k * BS : (k + 1) * BS, hw:] = lo

    def split_tiles(f):
        for t in range(n_row):
            hi, lo = split(tiles[f, t])
            th[f, t] = hi
            tl[f, t] = lo

    def split_panels(f):
        for j in range(nz):
            own = panels[f, j, pl.ds(pl.multiple_of(s * share, share), share), :]
            hi, lo = split(own.T)
            pth[f, j] = hi
            ptl[f, j] = lo
            hi, lo = split(panels[f, j].T)
            pfh[f, j] = hi
            pfl[f, j] = lo

    def mask_nodes():
        for f in range(fronts):
            for h in range(nh):
                cols = node_ids(bounds, f, h * hw, (half, hw), 1)
                for a in range(width // half):
                    same = node_ids(bounds, f, a * half, (half, hw), 0) == cols
                    at = (f, pl.ds(a * half, half), pl.ds(h * hw, hw))
                    masks[at] = same.astype(jnp.float32)

    def split_first():
        upper = pl.ds(pl.multiple_of(s * share, share), sh2)
        lower = pl.ds(pl.multiple_of(s * share + sh2 + z * e0, e0), e0)
        for j in range(nz):
            hi, lo = split(panels[0, j, upper, :].T)
            tah[:, j * sh2 : (j + 1) * sh2] = hi
            tal[:, j * sh2 : (j + 1) * sh2] = lo
        own = jnp.concatenate([panels[0, j, lower, :] for j in range(nz)], axis=0)
        hi, lo = split(own.T)
        tbh[...] = hi
        tbl[...] = lo

    along_x, along_row, along_z = {}, {}, {}
    to_core, to_plane, to_depth, back, to_half = {}, {}, {}, {}, {}

    def x_peers():
        for d in range(1, nx):
            to = lax.rem(s + d, nx)
            yield d, to, (r, z * nx + to)

    order = [divmod(n, n_row) for n in range(total_pieces)]
    order.remove((last - 1, n_row - 1))
    order.insert(order.index((last, n_row - 2)), (last - 1, n_row - 1))

    def piece_product(n):
        i, o = order[n]
        f, keep = i // nh, kept[i]
        both = dot(th[f, slots[o]], bm[i])
        low = dot(tl[f, slots[o]], bm[i, :, :hw])
        total = both[:, :hw] + (both[:, hw:] + low)
        if i > 0 and o == n_row - 1:
            own_u[i] = total
        if i > 0 and o == n_row - 2:
            par_s[i] = total
            along_row[i, "whole"] = mail.send(par_s.at[i], par_r.at[i], (partner, c))
        for to in range(nx):
            part[i, o, to, :keep] = total[to * share : to * share + keep]
        rows = pl.ds(0, keep)
        for d, to, peer in x_peers():
            along_x[n, d] = mail.send(
                part.at[i, o, to, rows], xbuf.at[i, o, d - 1, rows], peer
            )
        if i > 0:
            return
        for x in range(nx):
            for q in range(nz):
                at = x * share + sh2 + q * e0
                p0[q, o, x] = total[at : at + e0]
        if o == n_row - 1:
            for at in (1, 0):
                along_z["near", at] = mail.send(
                    p0.at[lax.rem(near + 2 * at, nz)], zn.at[at], (r, near * nx + s)
                )

    def piece_sum(n):
        i, o = order[n]
        keep = kept[i]
        total = part[i, o, s, :keep]
        for d in range(1, nx):
            along_x[n, d].wait_recv()
            total = total + xbuf[i, o, d - 1, :keep]
        if o == n_row - 1:
            rbuf[i][r, :keep] = total
        else:
            xs[i, o, :keep] = total
            rows = pl.ds(0, keep)
            along_row[i, o] = mail.send(
                xs.at[i, o, rows], rbuf[i].at[r, rows], (slots[o], c)
            )

    def first_far():
        along_z["near", 1].wait_recv()
        fs[...] = p0[far] + zn[1]
        along_z["far"] = mail.send(fs, zf, (r, far * nx + s))

    def first_x():
        along_z["near", 0].wait_recv()
        along_z["far"].wait_recv()
        for x in range(nx):
            for o in range(n_row):
                x0[x, o] = p0[z, o, x] + zn[0, o, x] + zf[o, x]
        for d, to, peer in x_peers():
            along_x["first", d] = mail.send(x0.at[to], x0r.at[d - 1], peer)

    def first_row():
        for d in range(1, nx):
            along_x["first", d].wait_recv()
        for o in range(n_row):
            total = x0[s, o]
            for d in range(1, nx):
                total = total + x0r[d - 1, o]
            if o == n_row - 1:
                rb0[r] = total
            else:
                rs0[o] = total
                along_row["first", o] = mail.send(rs0.at[o], rb0.at[r], (slots[o], c))

    def first_join():
        for o in range(n_row - 1):
            along_row["first", o].wait_recv()
        for j in range(nz):
            q0[j] = rb0[fb[0, r * per_owner + j] // rg]
        whole = jnp.concatenate([q0[j] for j in range(nz)], axis=0)
        diag_start(0, inner_product(whole, tbh, tbl) + inner0[...])
        zc[z] = q0[z]
        for d, to in enumerate(depth, 1):
            along_z["owner", d] = mail.send(q0.at[to], zc.at[z], (r, to * nx + s))

    def first_finish():
        for d in range(1, nz):
            along_z["owner", d].wait_recv()
        for q in range(nz):
            bsum[0, sh2 + q * e0 : sh2 + (q + 1) * e0, :hw] = zc[q]

    def inner_product(whole, left_hi, left_lo):
        hi, lo = split(whole)
        both = dot(left_hi[...], jnp.concatenate([hi, lo], axis=1))
        return both[:, :hw] + (both[:, hw:] + dot(left_lo[...], hi))

    def diag_start(i, inner):
        f, h = divmod(i, nh)
        ids = node_ids(bounds, f, 0, (half, hw), 0)
        same = ids == node_ids(bounds, f, h * hw, (half, hw), 1)
        packed = jnp.where(same, inner[:half], inner[half:])
        for e in range(groups):
            dpk[i, e] = packed[e * rows_each : (e + 1) * rows_each]
        if i in direct:
            for at, (e, peer) in enumerate(plane):
                to_plane[i, at] = mail.send(dpk.at[i, e], rsb.at[i, at], peer)
        else:
            to_core[i] = mail.send(
                dpk.at[i, pl.ds(other * half_groups, half_groups)], csb.at[i], (partner, c)
            )

    arrived = set()

    def row_wait(i, o):
        if (i, o) not in arrived:
            arrived.add((i, o))
            along_row[i, o].wait_recv()

    def position(f, g):
        at = jnp.int32(0)
        found = jnp.int32(0)
        for j in range(nz):
            hit = fb[f, r * per_owner + j] // rg == g
            at = jnp.where(hit, j, at)
            found = jnp.where(hit, 1, found)
        return at, found

    def diag_go(i):
        f = i // nh
        inner = jnp.zeros((width, hw), jnp.float32)
        along_row[i, "whole"].wait_recv()
        sources = [(r, own_u[i], pfh, pfl), (partner, par_r[i], pfh, pfl)]
        for o in range(n_row - 2):
            row_wait(i, o)
        for o in range(n_row - 2):
            sources.append((slots[o], rbuf[i][slots[o]], pth, ptl))
        for g, block, left_hi, left_lo in sources:
            j, found = position(f, g)
            if n_row != nz:
                block = jnp.where(found == 1, block, 0.0)
            inner = inner + inner_product(block, left_hi.at[f, j], left_lo.at[f, j])
        diag_start(i, inner)

    def z_diag(i):
        f, keep = i // nh, kept[i]
        for o in range(n_row - 1):
            row_wait(i, o)
        for j in range(nz):
            qs[i, j, :keep] = rbuf[i][fb[f, r * per_owner + j] // rg, :keep]
        if i == 0:
            whole = jnp.concatenate([qs[i, j, :keep] for j in range(nz)], axis=0)
            inner0[...] = inner_product(whole, tah, tal)

    def z_first(i, slots_sent=(1, 0)):
        rows = pl.ds(0, kept[i])
        for at in slots_sent:
            along_z[i, at] = mail.send(
                qs.at[i, lax.rem(near + 2 * at, nz), rows],
                zbuf.at[i, at, rows],
                (r, near * nx + s),
            )

    def z_second(i):
        keep = kept[i]
        along_z[i, 1].wait_recv()
        zs[i, :keep] = qs[i, far, :keep] + zbuf[i, 1, :keep]
        rows = pl.ds(0, keep)
        along_z[i, 2] = mail.send(zs.at[i, rows], zbuf.at[i, 2, rows], (r, far * nx + s))

    def diag_half(i):
        to_core[i].wait_recv()
        hs[i] = dpk[i, pl.ds(core * half_groups, half_groups)] + csb[i]
        for at, (e, peer) in enumerate(flat):
            to_plane[i, at] = mail.send(hs.at[i, e], rsb.at[i, at], peer)

    def diag_sum(i):
        if i in direct:
            total, count = dpk[i, mine], len(plane)
        else:
            total, count = hs[i, flat_mine], len(flat)
        for at in range(count):
            to_plane[i, at].wait_recv()
            total = total + rsb[i, at]
        zb[i, z] = total
        for d, to in enumerate(depth, 1):
            piece = zb.at[i, z]
            to_depth[i, d] = mail.send(piece, piece, (r, to * nx + s))

    def diag_back(i):
        for d in range(1, nz):
            to_depth[i, d].wait_recv()
        total = zb[i, 0]
        for j in range(1, nz):
            total = total + zb[i, j]
        pkall[i, mine] = total
        for at, (_, peer) in enumerate(plane if i in wide else flat):
            piece = pkall.at[i, mine]
            back[i, at] = mail.send(piece, piece, peer)

    def diag_share(i):
        for at in range(len(flat)):
            back[i, at].wait_recv()
        piece = pkall.at[i, pl.ds(core * half_groups, half_groups)]
        to_half[i] = mail.send(piece, piece, (partner, c))

    def finish(i):
        f, h = divmod(i, nh)
        keep = kept[i]
        along_z[i, 0].wait_recv()
        total = qs[i, z, :keep] + zbuf[i, 0, :keep]
        along_z[i, 2].wait_recv()
        bsum[f, :keep, h * hw : (h + 1) * hw] = total + zbuf[i, 2, :keep]

    def done(i):
        if i in wide:
            for at in range(len(plane)):
                back[i, at].wait_recv()
        else:
            to_half[i].wait_recv()

    barrier = pltpu.get_barrier_semaphore()
    peers = [peer for _, peer in plane] + [(r, to * nx + s) for to in depth]
    for peer in peers:
        pl.semaphore_signal(barrier, inc=1, device_id=peer, device_id_type=MESH)
    for copy in small:
        copy.wait()
    for i in range(chunks):
        w_pick(i)
    pl.semaphore_wait(barrier, len(peers))
    w_send(0)
    for f in range(fronts):
        split_tiles(f)
    for f in range(fronts):
        split_panels(f)
    w_send(1)
    w_relay(0)
    w_ready(0)
    for n in range(AHEAD):
        piece_product(n)
    w_relay(1)
    w_send(2)
    split_first()
    mask_nodes()

    tasks = {}

    def plan(n, task, *args):
        tasks.setdefault(n, []).append((task, args))

    plan(n_row - 1, first_far)
    plan(n_row - 1, w_send, last)
    for i in range(last):
        end = order.index((i, n_row - 1))
        at = end + 1 if i == 0 else end
        plan(at, z_diag, i)
        plan(at, z_first, i)
        if end + 3 < total_pieces:
            plan(end + 3 + (i == 0), z_second, i)
    plan(2 * n_row - 1, diag_go, 1)
    plan(2 * n_row + 1, diag_half, 1)
    plan(max(3 * n_row - 1, order.index((2, n_row - 1)) - AHEAD), diag_go, 2)
    if 2 not in direct:
        plan(3 * n_row + 1, diag_half, 2)
    plan(total_pieces - 2, diag_go, last)
    plan(total_pieces - 3, diag_sum, 1)
    plan(3 * n_row - 2, finish, 0)
    plan(3 * n_row - 2, first_row)
    plan(total_pieces - 3, first_join)
    for n in range(total_pieces):
        piece_sum(n)
        if n == 2 * n_row - 2:
            first_x()
        ahead = n + AHEAD
        if ahead < total_pieces:
            i = order[ahead][0]
            if i > 0 and order[ahead][1] == 0:
                if i == 2:
                    w_relay(2)
                if i == last:
                    w_relay(last)
                w_ready(i)
            piece_product(ahead)
        for task, args in tasks.get(n, []):
            task(*args)
    z_diag(last)
    if order.index((2, n_row - 1)) + 3 >= total_pieces:
        z_second(last - 1)
    diag_sum(2)
    diag_sum(0)
    z_first(last, (1,))
    diag_sum(last)
    diag_back(1)
    diag_back(2)
    diag_back(0)
    z_second(last)
    z_first(last, (0,))
    diag_share(1)
    diag_back(last)
    diag_share(2)
    diag_share(0)
    finish(1)
    finish(2)
    first_finish()
    finish(last)
    for i in range(chunks):
        done(i)
    mail.close()


def last_kernel(masks, bsum, pk, terms, border, diag, neg, full, sem):
    fronts, width = terms.shape[:2]
    half, hw = pk.shape[1:]
    neg[...] = -bsum[...]
    copies = [pltpu.make_async_copy(neg, border, sem.at[fronts])]
    copies[0].start()
    for f in range(fronts):
        for h in range(width // hw):
            for a in range(width // half):
                at = (f, pl.ds(a * half, half), pl.ds(h * hw, hw))
                full[at] = masks[at] * (terms[at] + pk[f * (width // hw) + h])
        copies.append(pltpu.make_async_copy(full.at[f], diag.at[f], sem.at[f]))
        copies[-1].start()
    for copy in copies:
        copy.wait()


def body(inverse, front_blocks, panels, diag_terms, bounds):
    n_row = lax.axis_size("row")
    n_col = lax.axis_size("col")
    rows_loc, cols_loc = inverse.shape
    rg = rows_loc // BS
    cg = cols_loc // BS
    fronts, kb = front_blocks.shape
    width = panels.shape[2]
    per_owner = kb // n_row
    nc = kb // n_col
    nz = per_owner
    nx = n_col // nz
    share = BS // nx
    nh = 2
    hw = width // nh
    half = width // 2
    chunks = fronts * nh
    groups = n_row * nx
    rows_each = half // groups
    sh2 = share // 2
    e0 = sh2 // nz
    dims = (fronts, kb, n_row, n_col, nz, nx, rg, cg, nh, hw)
    f32, bf16 = jnp.float32, jnp.bfloat16
    vmem = pl.BlockSpec(memory_space=pltpu.VMEM)
    anywhere = pl.BlockSpec(memory_space=pltpu.HBM)
    blocks = panels.reshape(fronts, per_owner, BS, width)

    tiles = pl.pallas_call(
        functools.partial(fetch_kernel, dims),
        out_shape=jax.ShapeDtypeStruct((fronts, n_row, BS, nc * BS), f32),
        in_specs=[anywhere, anywhere],
        out_specs=vmem,
        scratch_shapes=[
            pltpu.SMEM((fronts, kb), jnp.int32),
            pltpu.SemaphoreType.DMA(()),
            pltpu.SemaphoreType.DMA((fronts, n_row, nc)),
        ],
        compiler_params=pltpu.CompilerParams(vmem_limit_bytes=24 << 20),
    )(front_blocks, inverse)

    count = copies_of(dims)
    V = pltpu.VMEM
    bsum, pk, masks = pl.pallas_call(
        functools.partial(main_kernel, dims),
        out_shape=(
            jax.ShapeDtypeStruct((fronts, share, width), f32),
            jax.ShapeDtypeStruct((chunks, groups, rows_each, hw), f32),
            jax.ShapeDtypeStruct((fronts, width, width), f32),
        ),
        in_specs=[anywhere, anywhere, vmem, vmem],
        out_specs=(vmem, vmem, vmem),
        scratch_shapes=[
            pltpu.SMEM((fronts, kb), jnp.int32),
            pltpu.SMEM(bounds.shape, jnp.int32),
            V((fronts, n_row, BS, nc * BS), bf16),
            V((fronts, n_row, BS, nc * BS), bf16),
            V((chunks, nc * BS, 2 * hw), bf16),
            [V((n_row, BS, hw), f32)] * chunks,
            V((chunks, n_row, nx, share, hw), f32),
            V((chunks, n_row, nx - 1, share, hw), f32),
            V((chunks, n_row, share, hw), f32),
            [V((n_row, share, hw), f32)] * chunks,
            V((chunks, nz, share, hw), f32),
            V((chunks, 3, share, hw), f32),
            V((chunks, share, hw), f32),
            V((fronts, nz, width, share), bf16),
            V((fronts, nz, width, share), bf16),
            V((fronts, nz, width, BS), bf16),
            V((fronts, nz, width, BS), bf16),
            V((chunks, BS, hw), f32),
            V((chunks, BS, hw), f32),
            V((chunks, BS, hw), f32),
            V((nz, n_row, nx, e0, hw), f32),
            V((2, n_row, nx, e0, hw), f32),
            V((n_row, nx, e0, hw), f32),
            V((n_row, nx, e0, hw), f32),
            V((nx, n_row, e0, hw), f32),
            V((nx - 1, n_row, e0, hw), f32),
            V((n_row, e0, hw), f32),
            V((n_row, e0, hw), f32),
            V((nz, e0, hw), f32),
            V((nz, e0, hw), f32),
            V((width, hw), f32),
            V((width, nz * sh2), bf16),
            V((width, nz * sh2), bf16),
            V((width, nz * e0), bf16),
            V((width, nz * e0), bf16),
            V((chunks, groups, rows_each, hw), f32),
            V((chunks, groups // 2, rows_each, hw), f32),
            V((chunks, groups // 2, rows_each, hw), f32),
            V((chunks, groups - 1, rows_each, hw), f32),
            V((chunks, nz, rows_each, hw), f32),
            pltpu.SemaphoreType.DMA((2,)),
            pltpu.SemaphoreType.DMA((count,)),
            pltpu.SemaphoreType.DMA((count,)),
        ],
        compiler_params=pltpu.CompilerParams(
            collective_id=0,
            has_side_effects=True,
            vmem_limit_bytes=32 << 20,
        ),
    )(front_blocks, bounds, tiles, blocks)

    return pl.pallas_call(
        last_kernel,
        out_shape=(
            jax.ShapeDtypeStruct((fronts, share, width), f32),
            jax.ShapeDtypeStruct((fronts, width, width), f32),
        ),
        in_specs=[vmem, vmem, vmem, vmem],
        out_specs=(anywhere, anywhere),
        scratch_shapes=[
            V((fronts, share, width), f32),
            V((fronts, width, width), f32),
            pltpu.SemaphoreType.DMA((fronts + 1,)),
        ],
        compiler_params=pltpu.CompilerParams(vmem_limit_bytes=16 << 20),
    )(masks, bsum, pk.reshape(chunks, half, hw), diag_terms)


def solution(mesh):
    placed = (P("row", "col"), P(), P(None, "row", None), P(), P())
    return jax.shard_map(
        body,
        mesh=mesh,
        in_specs=placed,
        out_specs=(P(None, ("row", "col"), None), P()),
        check_vma=False,
    )
```
